512 devices in a mesh: sims: 32 (over z_lo, y, core), rows: 16 (over x, z_hi).
Axes of the slice: x: 4, y: 8, z: 8 (z_hi: 4, z_lo: 2; z = z_hi * 2 + z_lo), core: 2. Of those that a mesh axis runs over, the one named last changes fastest.
Arguments:
- maps: float32 [32, 1024, 2048], P('sims', 'rows'), may hold values from -6 to 6
- weight: float32 [1024, 2048], P('rows'), may hold values from 0.1 to 1.5
- beam: float32 [65], replicated, may hold values from 0.05 to 1
- pair_one: int32 [32], replicated, may hold values from 0 to 31, each once
- pair_two: int32 [32], replicated, may hold values from 0 to 31, each once
- owner: int32 [32], replicated, may hold values from 0 to 7
Outputs:
- estimate: float32 [32, 1024, 2048], P('sims', 'rows')
- mean_field: float32 [8, 1024, 2048], P(None, 'rows', 'sims')
The draws below stay inside these ranges and needn't reach their ends.
Inputs may be any that keep to these rules, and one draw needn't show every extreme that they name: `pair_one`: each a permutation of the evolutions. `pair_two`: each a permutation of the evolutions.
All inputs are finite; a program needn't handle non-finite values.
Results may differ from the reference program's by a relative error of at most 0.00016.
Values sent between devices are 32-bit elements; how exact they have to be, the bound alone decides.
A program may use at most 64 MiB of HBM per device.

```python
import math
import jax
import jax.numpy as jnp
from jax import lax

NCOL = 2048
TAPS = 65
ITERS = 3
OWNERS = 8
SIMS = 32
NROWS = 1024


def plant(values, rng, least, high):
    spot = [jax.random.randint(jax.random.fold_in(rng, axis), (), 0, length) for axis, length in enumerate(values.shape)]
    widest = values.shape.index(max(values.shape))
    neighbour = spot[:widest] + [(spot[widest] + 1) % values.shape[widest]] + spot[widest + 1:]
    return values.at[tuple(spot)].set(least).at[tuple(neighbour)].set(high)


def level_of(key, shape, cuts, least, high):
    def one(axis_at, blocks):
        heights = jax.random.uniform(jax.random.fold_in(jax.random.fold_in(key, 6), axis_at), (blocks,), jnp.float32, least / len(cuts), high / len(cuts))
        return jnp.repeat(jnp.exp(heights), shape[axis_at] // blocks).reshape((-1,) + (1,) * (len(shape) - axis_at - 1))

    loudness = one(*cuts[0])
    for cut in cuts[1:]:
        loudness = loudness * one(*cut)
    return loudness


def scatter_about(rng, shape, deviation, most, pieces=(), kind=jnp.bfloat16):
    entries = deviation * jax.random.normal(rng, shape, jnp.float32)
    if pieces:
        entries = entries * level_of(rng, shape, pieces, -0.22, 0.18)
    return jnp.clip(entries, -most, most).astype(kind)


def setup_inputs(seed: int = 0) -> dict:
    keys = jax.random.split(jax.random.key(seed), 7)
    return {
        "maps": scatter_about(keys[0], (SIMS, NROWS, NCOL), 1.0, 6.0, ((0, 32), (1, 16)), jnp.float32),
        "weight": jnp.clip(jnp.exp(math.log(1.5) - 2.7080502 * jax.random.uniform(keys[1], (NROWS, NCOL), jnp.float32) ** level_of(keys[1], (NROWS, NCOL), ((0, 16),), -0.2, 0.2)), 0.1, 1.5),
        "beam": jnp.clip(jnp.exp(jax.random.uniform(keys[2], (TAPS,), jnp.float32, math.log(0.05), math.log(1.0))), 0.05, 1.0),
        "pair_one": jax.random.permutation(keys[3], SIMS).astype(jnp.int32),
        "pair_two": jax.random.permutation(keys[4], SIMS).astype(jnp.int32),
        "owner": plant(jax.random.randint(keys[5], (SIMS,), 0, OWNERS), jax.random.fold_in(keys[5], 1), 0, OWNERS - 1).astype(jnp.int32),
    }


ridge_term = 0.5
step_size = 0.6


def smear(field, coeffs, axis):
    length = field.shape[axis]
    extent = coeffs.shape[0]
    padded_len = length + extent - 1
    spectrum = jnp.fft.rfft(field, n=padded_len, axis=axis)
    response = jnp.fft.rfft(coeffs[::-1], n=padded_len)
    layout = [1, 1]
    layout[axis] = response.shape[0]
    complete = jnp.fft.irfft(spectrum * response.reshape(layout), n=padded_len, axis=axis)
    offset = (extent - 1) // 2
    return lax.slice_in_dim(complete, offset, offset + length, axis=axis)


def blur(field, coeffs):
    return smear(smear(field, coeffs, 1), coeffs, 0)


def diff_rows(field):
    padded = jnp.pad(field, ((1, 1), (0, 0)))
    return 0.5 * (padded[2:] - padded[:-2])


def diff_cols(field):
    padded = jnp.pad(field, ((0, 0), (1, 1)))
    return 0.5 * (padded[:, 2:] - padded[:, :-2])


def divergence(own_map, partner):
    return diff_rows(own_map * diff_rows(partner)) + diff_cols(own_map * diff_cols(partner))


def reference(maps, weight, beam, pair_one, pair_two, owner):
    kernel = beam / jnp.sum(beam)
    flipped = kernel[::-1]

    def filter_one(single):
        source = blur(weight * single, flipped)
        current = step_size * source
        for iteration in range(ITERS):
            applied = ridge_term * current + blur(weight * blur(current, kernel), flipped)
            current = current + step_size * (source - applied)
        return current

    filtered = lax.map(filter_one, maps)

    def estimate_one(index):
        own_map = filtered[index]
        first = filtered[pair_one[index]]
        second = filtered[pair_two[index]]
        return 2.0 * divergence(own_map, first) - divergence(own_map, second)

    estimate = lax.map(estimate_one, jnp.arange(SIMS, dtype=jnp.int32))
    sums = jax.ops.segment_sum(estimate, owner, num_segments=OWNERS)
    counts = jax.ops.segment_sum(jnp.ones((SIMS,), jnp.float32), owner, num_segments=OWNERS)
    mean_field = sums / jnp.maximum(counts, 1.0)[:, None, None]
    return estimate, mean_field
```

```python
import jax
import jax.numpy as jnp
from jax import lax
from jax.experimental import pallas as pl
from jax.experimental.pallas import tpu as pltpu
from jax.sharding import Mesh
from jax.sharding import PartitionSpec as P

TAPS = 65
ITERS = 3
OWNERS = 8
STEPS = 2 * ITERS + 1
REACH = 32
LANES = 128
WIDE = 256
WINDOW = 512
ridge_term = 0.5
step_size = 0.6
F32 = jnp.float32
BF16 = jnp.bfloat16
MESH = pl.DeviceIdType.MESH


def halves(x):
    high = x.astype(BF16)
    return high, (x - high.astype(F32)).astype(BF16)


def dot(a, b):
    return jnp.dot(a, b, preferred_element_type=F32)


def filter_kernel(maps_ref, weight_ref, taps_ref, out_ref, f_ref, source_ref, h_ref, acc_ref, top_ref, bottom_ref, rim_out, rim_in, across_h, across_l, down_own, down_rim, x_h, x_l, own_ref, rim_ref, edge_ref, send_sem, recv_sem, rim_send, rim_recv):
    count = lax.axis_size("rows")
    me = lax.axis_index("rows")
    above, below = {"rows": me - 1}, {"rows": me + 1}
    has_above, has_below = me > 0, me < count - 1
    rows, cols = f_ref.shape
    blocks, pairs = cols // LANES, cols // WIDE

    barrier = pltpu.get_barrier_semaphore()

    @pl.when(has_above)
    def _():
        pl.semaphore_signal(barrier, inc=1, device_id=above, device_id_type=MESH)

    @pl.when(has_below)
    def _():
        pl.semaphore_signal(barrier, inc=1, device_id=below, device_id_type=MESH)

    for way in range(2):
        line = jnp.broadcast_to(taps_ref[1 - way : 2 - way, :], (WINDOW, WINDOW))
        table = pltpu.roll(line, WINDOW - 160, 1, stride=1, stride_axis=0)[:, :WIDE]
        high, low = halves(table)
        across_h[way] = high
        across_l[way] = low
        line = jnp.broadcast_to(taps_ref[way : way + 1, :LANES], (rows, LANES))
        inside = pltpu.roll(line, LANES - REACH, 1, stride=1, stride_axis=0)
        over = pltpu.roll(line, 64, 1, stride=1, stride_axis=0)
        under = pltpu.roll(line, 0, 1, stride=1, stride_axis=0)
        place = lax.broadcasted_iota(jnp.int32, (rows, LANES), 1)
        rim = jnp.where(place < 96, over, under)
        high, low = halves(inside[:, :64])
        down_own[way] = jnp.concatenate([high, low, high], axis=1)
        high, low = halves(rim[:, 64:])
        down_rim[way] = jnp.concatenate([high, low, high], axis=1)

    nothing = jnp.zeros((rows, LANES), BF16)
    for ref in (x_h, x_l):
        ref[0:rows, 0:LANES] = nothing
        ref[(pairs - 1) * rows : pairs * rows, 3 * LANES : 4 * LANES] = nothing

    @pl.when(jnp.logical_not(has_above))
    def _():
        top_ref[...] = jnp.zeros_like(top_ref)
        rim_in[0] = jnp.zeros_like(rim_in[0])

    @pl.when(jnp.logical_not(has_below))
    def _():
        bottom_ref[...] = jnp.zeros_like(bottom_ref)
        rim_in[1] = jnp.zeros_like(rim_in[1])

    def put(block, value):
        high, low = halves(value)
        for pair in range(pairs):
            place = block - 2 * pair + 1
            if 0 <= place < 4:
                spot = (slice(pair * rows, (pair + 1) * rows), slice(place * LANES, (place + 1) * LANES))
                x_h[spot] = high
                x_l[spot] = low

    def up_copy(step):
        return pltpu.make_async_remote_copy(
            src_ref=h_ref.at[0:REACH], dst_ref=bottom_ref.at[step], send_sem=send_sem.at[0, step], recv_sem=recv_sem.at[1, step], device_id=above, device_id_type=MESH
        )

    def down_copy(step):
        return pltpu.make_async_remote_copy(
            src_ref=h_ref.at[REACH : 2 * REACH], dst_ref=top_ref.at[step], send_sem=send_sem.at[1, step], recv_sem=recv_sem.at[0, step], device_id=below, device_id_type=MESH
        )

    def half_step(step, way):
        table_h, table_l = across_h[way], across_l[way]
        for pair in range(pairs):
            high, low = x_h[pair * rows : (pair + 1) * rows], x_l[pair * rows : (pair + 1) * rows]
            both = dot(jnp.concatenate([high, low], axis=0), table_h)
            value = both[:rows] + both[rows:] + dot(high, table_l)
            h_ref[:, pair * WIDE : (pair + 1) * WIDE] = value

        @pl.when(has_above)
        def _():
            up_copy(step).start()

        @pl.when(has_below)
        def _():
            down_copy(step).start()

        high, low = halves(h_ref[...])
        own_ref[0:rows] = high
        own_ref[rows : 2 * rows] = high
        own_ref[2 * rows : 3 * rows] = low
        acc_ref[...] = dot(down_own[way], own_ref[...])

        @pl.when(has_above)
        def _():
            down_copy(step).wait_recv()

        @pl.when(has_below)
        def _():
            up_copy(step).wait_recv()

        for at, ref in ((0, top_ref), (REACH, bottom_ref)):
            high, low = halves(ref[step])
            rim_ref[at : at + REACH] = high
            rim_ref[rows + at : rows + at + REACH] = high
            rim_ref[2 * rows + at : 2 * rows + at + REACH] = low
        acc_ref[...] += dot(down_rim[way], rim_ref[...])

        @pl.when(has_above)
        def _():
            up_copy(step).wait_send()

        @pl.when(has_below)
        def _():
            down_copy(step).wait_send()

    spans = [slice(b * LANES, (b + 1) * LANES) for b in range(blocks)]
    for b in range(blocks):
        put(b, weight_ref[:, spans[b]] * maps_ref[:, spans[b]])

    inner = jnp.logical_and(has_above, has_below)

    @pl.when(inner)
    def _():
        pl.semaphore_wait(barrier, 2)

    @pl.when(jnp.logical_not(inner))
    def _():
        pl.semaphore_wait(barrier, 1)

    half_step(0, 1)
    for b in range(blocks):
        first = step_size * acc_ref[:, spans[b]]
        source_ref[:, spans[b]] = first
        f_ref[:, spans[b]] = first
        put(b, first)

    def iteration(turn, carry):
        half_step(2 * turn + 1, 0)
        for b in range(blocks):
            put(b, weight_ref[:, spans[b]] * acc_ref[:, spans[b]])
        half_step(2 * turn + 2, 1)
        for b in range(blocks):
            value = (1.0 - step_size * ridge_term) * f_ref[:, spans[b]] + source_ref[:, spans[b]] - step_size * acc_ref[:, spans[b]]
            f_ref[:, spans[b]] = value
            put(b, value)
        return carry

    lax.fori_loop(0, ITERS, iteration, 0)

    quarter = cols // 4
    for k in range(4):
        rim_out[0, 2 * k : 2 * k + 2, :] = f_ref[0:2, k * quarter : (k + 1) * quarter]
        rim_out[1, 2 * k : 2 * k + 2, :] = f_ref[rows - 2 : rows, k * quarter : (k + 1) * quarter]

    def rim_up():
        return pltpu.make_async_remote_copy(src_ref=rim_out.at[0], dst_ref=rim_in.at[1], send_sem=rim_send.at[0], recv_sem=rim_recv.at[1], device_id=above, device_id_type=MESH)

    def rim_down():
        return pltpu.make_async_remote_copy(src_ref=rim_out.at[1], dst_ref=rim_in.at[0], send_sem=rim_send.at[1], recv_sem=rim_recv.at[0], device_id=below, device_id_type=MESH)

    @pl.when(has_above)
    def _():
        rim_up().start()

    @pl.when(has_below)
    def _():
        rim_down().start()

    for b in range(blocks):
        turned = f_ref[:, spans[b]].T
        for k, lane in enumerate((0, 1, 126, 127)):
            edge_ref[k, b : b + 1, :] = turned[lane : lane + 1, :]
    zero, one, two, three = (edge_ref[k] for k in range(4))
    gap = jnp.zeros((1, rows), F32)
    before = [jnp.concatenate([gap, x[:-1]], axis=0) for x in (two, three)]
    after = [jnp.concatenate([x[1:], gap], axis=0) for x in (zero, one)]
    blank = jnp.zeros((blocks, REACH), F32)
    for h in range(2):
        part = slice(h * REACH, (h + 1) * REACH)
        left = jnp.concatenate([before[0][:, part], before[1][:, part], zero[:, part], blank], axis=1)
        right = jnp.concatenate([three[:, part], after[0][:, part], after[1][:, part], blank], axis=1)
        for b in range(blocks):
            out_ref[2 * b + h, 34:35, :] = left[b : b + 1]
            out_ref[2 * b + h, 35:36, :] = right[b : b + 1]

    for b in range(blocks):
        for h in range(2):
            at = 2 * b + h
            out_ref[at, 0:REACH, :] = f_ref[h * REACH : (h + 1) * REACH, spans[b]]
            out_ref[at, 36:38, :] = jnp.zeros((2, LANES), F32)
        out_ref[2 * b, 32:34, :] = f_ref[REACH : REACH + 2, spans[b]]
        out_ref[2 * b + 1, 38:40, :] = f_ref[REACH - 2 : REACH, spans[b]]

    @pl.when(has_above)
    def _():
        rim_down().wait_recv()

    @pl.when(has_below)
    def _():
        rim_up().wait_recv()

    for b in range(blocks):
        k, lane = b // 4, (b % 4) * LANES
        out_ref[2 * b, 38:40, :] = rim_in[0, 2 * k : 2 * k + 2, lane : lane + LANES]
        out_ref[2 * b + 1, 32:34, :] = rim_in[1, 2 * k : 2 * k + 2, lane : lane + LANES]

    @pl.when(has_above)
    def _():
        rim_up().wait_send()

    @pl.when(has_below)
    def _():
        rim_down().wait_send()


def filtered_pieces(maps, weight, taps):
    rows, cols = maps.shape
    pieces = cols // LANES * 2
    vmem = pl.BlockSpec(memory_space=pltpu.VMEM)
    stacked = (cols // WIDE * rows, WINDOW)
    return pl.pallas_call(
        filter_kernel,
        out_shape=jax.ShapeDtypeStruct((pieces, REACH + 8, LANES), F32),
        in_specs=[vmem] * 3,
        out_specs=vmem,
        scratch_shapes=[
            pltpu.VMEM((rows, cols), F32),
            pltpu.VMEM((rows, cols), F32),
            pltpu.VMEM((rows, cols), F32),
            pltpu.VMEM((rows, cols), F32),
            pltpu.VMEM((STEPS, REACH, cols), F32),
            pltpu.VMEM((STEPS, REACH, cols), F32),
            pltpu.VMEM((2, 8, cols // 4), F32),
            pltpu.VMEM((2, 8, cols // 4), F32),
            pltpu.VMEM((2, WINDOW, WIDE), BF16),
            pltpu.VMEM((2, WINDOW, WIDE), BF16),
            pltpu.VMEM((2, rows, 3 * rows), BF16),
            pltpu.VMEM((2, rows, 3 * rows), BF16),
            pltpu.VMEM(stacked, BF16),
            pltpu.VMEM(stacked, BF16),
            pltpu.VMEM((3 * rows, cols), BF16),
            pltpu.VMEM((3 * rows, cols), BF16),
            pltpu.VMEM((4, cols // LANES, rows), F32),
            pltpu.SemaphoreType.DMA((2, STEPS)),
            pltpu.SemaphoreType.DMA((2, STEPS)),
            pltpu.SemaphoreType.DMA((2,)),
            pltpu.SemaphoreType.DMA((2,)),
        ],
        compiler_params=pltpu.CompilerParams(collective_id=0, has_side_effects=True),
    )(maps, weight, taps)


def estimate_kernel(one_ref, two_ref, owner_ref, pieces_ref, est_ref, mean_ref, line_ref, flow_ref):
    sims = pieces_ref.shape[0]
    line_ref[...] = jnp.zeros_like(line_ref)
    for s in range(sims):
        own = pieces_ref[s, 34:36, :]
        partner = 2.0 * pieces_ref[one_ref[s], 34:36, :] - pieces_ref[two_ref[s], 34:36, :]
        for side in range(2):
            line_ref[side, s : s + 1, :] = own[side : side + 1]
            line_ref[2 + side, s : s + 1, :] = partner[side : side + 1]
    own_l, own_r, g_l, g_r = (line_ref[k].T for k in range(4))

    def col(x, k):
        return x[k * REACH : (k + 1) * REACH, :]

    flow_ref[0] = 0.5 * col(own_l, 1) * (col(g_l, 2) - col(g_l, 0))
    flow_ref[1] = 0.5 * col(own_r, 1) * (col(g_r, 2) - col(g_r, 0))
    flow_ref[2] = col(g_l, 1)
    flow_ref[3] = col(g_r, 1)
    lane = lax.broadcasted_iota(jnp.int32, (REACH, LANES), 1)
    first, last = lane == 0, lane == LANES - 1
    depth = REACH + 8
    mean_ref[...] = jnp.zeros_like(mean_ref)
    for s in range(sims):
        f = pieces_ref[s]
        g = 2.0 * pieces_ref[one_ref[s]] - pieces_ref[two_ref[s]]
        p = f * (pltpu.roll(g, depth - 1, 0) - pltpu.roll(g, 1, 0))
        by_rows = (pltpu.roll(p, depth - 1, 0) - pltpu.roll(p, 1, 0))[:REACH]
        f, g = f[:REACH], g[:REACH]

        def vector(k):
            return jnp.broadcast_to(flow_ref[k, :, s : s + 1], (REACH, LANES))

        ahead = jnp.where(last, vector(3), pltpu.roll(g, LANES - 1, 1))
        behind = jnp.where(first, vector(2), pltpu.roll(g, 1, 1))
        q = 0.5 * f * (ahead - behind)
        ahead = jnp.where(last, vector(1), pltpu.roll(q, LANES - 1, 1))
        behind = jnp.where(first, vector(0), pltpu.roll(q, 1, 1))
        value = 0.25 * by_rows + 0.5 * (ahead - behind)
        est_ref[s] = value
        for o in range(OWNERS):
            mean_ref[o] += jnp.where(owner_ref[s] == o, value, 0.0)
    for o in range(OWNERS):
        tally = jnp.int32(0)
        for s in range(sims):
            tally = tally + (owner_ref[s] == o).astype(jnp.int32)
        mean_ref[o] = mean_ref[o] / jnp.full((REACH, LANES), jnp.maximum(tally, 1).astype(F32))


def estimates(pieces, pair_one, pair_two, owner):
    sims = pieces.shape[0]
    vmem, smem = pl.BlockSpec(memory_space=pltpu.VMEM), pl.BlockSpec(memory_space=pltpu.SMEM)
    return pl.pallas_call(
        estimate_kernel,
        out_shape=(jax.ShapeDtypeStruct((sims, REACH, LANES), F32), jax.ShapeDtypeStruct((OWNERS, REACH, LANES), F32)),
        in_specs=[smem] * 3 + [vmem],
        out_specs=(vmem, vmem),
        scratch_shapes=[pltpu.VMEM((4, LANES, LANES), F32), pltpu.VMEM((4, REACH, LANES), F32)],
    )(pair_one, pair_two, owner, pieces)


def body(maps, weight, beam, pair_one, pair_two, owner):
    rows, cols = weight.shape
    kernel = beam / jnp.sum(beam)
    taps = jnp.pad(jnp.stack([kernel, kernel[::-1]]), ((0, 6), (0, WINDOW - TAPS)))
    pieces = filtered_pieces(maps[0], weight, taps)
    pieces = lax.all_to_all(pieces, ("chips", "core"), split_axis=0, concat_axis=0, tiled=True)
    est, mean = estimates(pieces, pair_one, pair_two, owner)
    est = lax.all_to_all(est, ("chips", "core"), split_axis=0, concat_axis=0, tiled=True)
    est = est.reshape(cols // LANES, 2, REACH, LANES).transpose(1, 2, 0, 3).reshape(1, rows, cols)
    mean = lax.all_to_all(mean, "core", split_axis=2, concat_axis=1, tiled=True)
    return est, mean


def solution(mesh):
    split = Mesh(mesh.devices.reshape(16, 2, mesh.shape["rows"]), ("chips", "core", "rows"))
    sims = ("chips", "core")
    return jax.shard_map(
        body,
        mesh=split,
        in_specs=(P(sims, "rows", None), P("rows", None), P(), P(), P(), P()),
        out_specs=(P(sims, "rows", None), P(None, "rows", sims)),
        check_vma=False,
    )
```

```python
import jax
import jax.numpy as jnp
from jax import lax
from jax.experimental import pallas as pl
from jax.experimental.pallas import tpu as pltpu
from jax.sharding import Mesh
from jax.sharding import PartitionSpec as P

TAPS = 65
ITERS = 3
OWNERS = 8
STEPS = 2 * ITERS + 1
REACH = 32
LANES = 128
WIDE = 256
WINDOW = 512
ridge_term = 0.5
step_size = 0.6
F32 = jnp.float32
BF16 = jnp.bfloat16
MESH = pl.DeviceIdType.MESH


def halves(x):
    high = x.astype(BF16)
    return high, (x - high.astype(F32)).astype(BF16)


def dot(a, b):
    return jnp.dot(a, b, preferred_element_type=F32)


def whole_kernel(one_ref, two_ref, owner_ref, maps_ref, weight_ref, beam_ref, result_ref, mean_ref, taps_ref, f_ref, source_ref, h_ref, top_ref, bottom_ref, rim_in, across_h, across_l, down, x_h, x_l, ext_ref, edge_ref, out_ref, got_ref, line_ref, flow_ref, est_ref, sums_ref, other_ref, send_sem, recv_sem, rim_send, rim_recv, deal_send, deal_recv, home_send, home_recv, mean_send, mean_recv):
    count = lax.axis_size("rows")
    me = lax.axis_index("rows")
    above, below = {"rows": me - 1}, {"rows": me + 1}
    has_above, has_below = me > 0, me < count - 1
    rows, cols = f_ref.shape
    blocks, pairs = cols // LANES, cols // WIDE

    sims = got_ref.shape[0]
    half = lax.axis_index("core")
    mine = 2 * lax.axis_index("chips") + half

    def peer(offset):
        other = lax.rem(mine + offset, sims)
        return other, {"chips": other // 2, "core": other % 2}

    barrier = pltpu.get_barrier_semaphore()

    def greet(offset, carry):
        pl.semaphore_signal(barrier, inc=1, device_id=peer(offset)[1], device_id_type=MESH)
        return carry

    lax.fori_loop(1, sims, greet, 0)

    @pl.when(has_above)
    def _():
        pl.semaphore_signal(barrier, inc=1, device_id=above, device_id_type=MESH)

    @pl.when(has_below)
    def _():
        pl.semaphore_signal(barrier, inc=1, device_id=below, device_id_type=MESH)

    taps_ref[...] = jnp.zeros_like(taps_ref)
    taps_ref[0:1, :TAPS] = beam_ref[...]
    taps = taps_ref[0:1, :] / jnp.sum(taps_ref[0:1, :], axis=1, keepdims=True)
    taps_ref[0:1, :] = taps
    square = (LANES, LANES)
    turned = jnp.broadcast_to(taps[:, :LANES], square).T
    places = lax.broadcasted_iota(jnp.int32, square, 0) + lax.broadcasted_iota(jnp.int32, square, 1)
    taps_ref[1:2, :LANES] = jnp.sum(jnp.where(places == TAPS - 1, turned, 0.0), axis=0, keepdims=True)

    def tables(way):
        line = jnp.broadcast_to(taps_ref[1 - way : 2 - way, :], (WINDOW, WINDOW))
        table = pltpu.roll(line, WINDOW - 160, 1, stride=1, stride_axis=0)[:, :WIDE]
        high, low = halves(table)
        across_h[way] = high
        across_l[way] = low
        line = jnp.broadcast_to(taps_ref[way : way + 1, :LANES], (rows, LANES))
        inside = pltpu.roll(line, LANES - REACH, 1, stride=1, stride_axis=0)
        over = pltpu.roll(line, 64, 1, stride=1, stride_axis=0)
        under = pltpu.roll(line, 0, 1, stride=1, stride_axis=0)
        place = lax.broadcasted_iota(jnp.int32, (rows, LANES), 1)
        rim = jnp.where(place < 96, over, under)
        high, low = halves(inside[:, :64])
        rim_h, rim_l = halves(rim[:, 64:])
        down[way] = jnp.concatenate([high, low, high, rim_h, rim_l, rim_h], axis=1)

    nothing = jnp.zeros((rows, LANES), BF16)
    for ref in (x_h, x_l):
        ref[0, :, 0:LANES] = nothing
        ref[pairs - 1, :, 3 * LANES : 4 * LANES] = nothing

    tops = (192, 256, 320)
    bottoms = (224, 288, 352)
    empty = jnp.zeros((pairs, REACH, WIDE), BF16)

    @pl.when(jnp.logical_not(has_above))
    def _():
        for at in tops:
            ext_ref[:, at : at + REACH, :] = empty
        rim_in[0] = jnp.zeros_like(rim_in[0])

    @pl.when(jnp.logical_not(has_below))
    def _():
        for at in bottoms:
            ext_ref[:, at : at + REACH, :] = empty
        rim_in[1] = jnp.zeros_like(rim_in[1])

    def put(block, value):
        high, low = halves(value)
        for pair in range(pairs):
            place = block - 2 * pair + 1
            if 0 <= place < 4:
                x_h[pair, :, place * LANES : (place + 1) * LANES] = high
                x_l[pair, :, place * LANES : (place + 1) * LANES] = low

    def up_copy(step, parity, pair):
        return pltpu.make_async_remote_copy(
            src_ref=h_ref.at[parity, pair, 0:REACH],
            dst_ref=bottom_ref.at[step, pair],
            send_sem=send_sem.at[0, step, pair],
            recv_sem=recv_sem.at[1, step, pair],
            device_id=above,
            device_id_type=MESH,
        )

    def down_copy(step, parity, pair):
        return pltpu.make_async_remote_copy(
            src_ref=h_ref.at[parity, pair, REACH : 2 * REACH],
            dst_ref=top_ref.at[step, pair],
            send_sem=send_sem.at[1, step, pair],
            recv_sem=recv_sem.at[0, step, pair],
            device_id=below,
            device_id_type=MESH,
        )

    def sent(step, parity, pair):
        @pl.when(has_above)
        def _():
            up_copy(step, parity, pair).wait_send()

        @pl.when(has_below)
        def _():
            down_copy(step, parity, pair).wait_send()

    def across(step, parity, way, pair, waits=True):
        if waits:
            sent(step - 2, parity, pair)
        high, low = x_h[pair], x_l[pair]
        both = dot(jnp.concatenate([high, low], axis=0), across_h[way])
        value = both[:rows] + both[rows:] + dot(high, across_l[way])
        h_ref[parity, pair] = value

        @pl.when(has_above)
        def _():
            up_copy(step, parity, pair).start()

        @pl.when(has_below)
        def _():
            down_copy(step, parity, pair).start()

        high, low = halves(value)
        ext_ref[pair, 0:rows] = high
        ext_ref[pair, rows : 2 * rows] = high
        ext_ref[pair, 2 * rows : 3 * rows] = low

    def downward(step, parity, way, pair):
        @pl.when(has_above)
        def _():
            down_copy(step, parity, pair).wait_recv()
            high, low = halves(top_ref[step, pair])
            for at, part in zip(tops, (high, high, low)):
                ext_ref[pair, at : at + REACH] = part

        @pl.when(has_below)
        def _():
            up_copy(step, parity, pair).wait_recv()
            high, low = halves(bottom_ref[step, pair])
            for at, part in zip(bottoms, (high, high, low)):
                ext_ref[pair, at : at + REACH] = part

        return dot(down[way], ext_ref[pair])

    spans = [slice(b * LANES, (b + 1) * LANES) for b in range(blocks)]
    tables(1)
    for b in range(blocks):
        put(b, weight_ref[:, spans[b]] * maps_ref[:, spans[b]])

    inner = jnp.logical_and(has_above, has_below)

    @pl.when(inner)
    def _():
        pl.semaphore_wait(barrier, sims + 1)

    @pl.when(jnp.logical_not(inner))
    def _():
        pl.semaphore_wait(barrier, sims)

    for p in range(pairs):
        across(0, 0, 1, p, waits=False)
    tables(0)

    def sweep(step, parity, way, use, after):
        for p in range(pairs):
            total = downward(step, parity, way, p)
            for k in range(2):
                use(2 * p + k, total[:, k * LANES : (k + 1) * LANES])
            if after is not None:
                if p > 0:
                    after(p - 1)
                if p == pairs - 1:
                    after(p)

    def begin(b, total):
        first = step_size * total
        source_ref[:, spans[b]] = first
        f_ref[:, spans[b]] = first
        put(b, first)

    def weigh(b, total):
        put(b, weight_ref[:, spans[b]] * total)

    def renew(b, total):
        value = (1.0 - step_size * ridge_term) * f_ref[:, spans[b]] + source_ref[:, spans[b]] - step_size * total
        f_ref[:, spans[b]] = value
        return value

    sweep(0, 0, 1, begin, lambda p: across(1, 1, 0, p, waits=False))

    def iteration(turn, carry):
        step = 2 * turn + 1
        sweep(step, 1, 0, weigh, lambda p: across(step + 1, 0, 1, p))
        sweep(step + 1, 0, 1, lambda b, total: put(b, renew(b, total)), lambda p: across(step + 2, 1, 0, p))
        return carry

    lax.fori_loop(0, ITERS - 1, iteration, 0)
    last = 2 * ITERS - 1
    sweep(last, 1, 0, weigh, lambda p: across(last + 1, 0, 1, p))

    def rim_up(pair):
        return pltpu.make_async_remote_copy(
            src_ref=f_ref.at[0:8, pair * WIDE : (pair + 1) * WIDE],
            dst_ref=rim_in.at[1, pair],
            send_sem=rim_send.at[0, pair],
            recv_sem=rim_recv.at[1, pair],
            device_id=above,
            device_id_type=MESH,
        )

    def rim_down(pair):
        return pltpu.make_async_remote_copy(
            src_ref=f_ref.at[rows - 8 : rows, pair * WIDE : (pair + 1) * WIDE],
            dst_ref=rim_in.at[0, pair],
            send_sem=rim_send.at[1, pair],
            recv_sem=rim_recv.at[0, pair],
            device_id=below,
            device_id_type=MESH,
        )

    def finish(b, total):
        value = renew(b, total)
        if b % 2 == 1:
            pair = b // 2

            @pl.when(has_above)
            def _():
                rim_up(pair).start()

            @pl.when(has_below)
            def _():
                rim_down(pair).start()

        for h in range(2):
            out_ref[2 * b + h, 0:REACH, :] = value[h * REACH : (h + 1) * REACH]
            out_ref[2 * b + h, 36:38, :] = jnp.zeros((2, LANES), F32)
        out_ref[2 * b, 32:34, :] = value[REACH : REACH + 2]
        out_ref[2 * b + 1, 38:40, :] = value[REACH - 2 : REACH]
        turned = value.T
        for k, lane in enumerate((0, 1, 126, 127)):
            edge_ref[k, b : b + 1, :] = turned[lane : lane + 1, :]

    sweep(last + 1, 0, 1, finish, None)

    zero, one, two, three = (edge_ref[k] for k in range(4))
    gap = jnp.zeros((1, rows), F32)
    before = [jnp.concatenate([gap, x[:-1]], axis=0) for x in (two, three)]
    after = [jnp.concatenate([x[1:], gap], axis=0) for x in (zero, one)]
    blank = jnp.zeros((blocks, REACH), F32)
    for h in range(2):
        part = slice(h * REACH, (h + 1) * REACH)
        left = jnp.concatenate([before[0][:, part], before[1][:, part], zero[:, part], blank], axis=1)
        right = jnp.concatenate([three[:, part], after[0][:, part], after[1][:, part], blank], axis=1)
        for b in range(blocks):
            out_ref[2 * b + h, 34:35, :] = left[b : b + 1]
            out_ref[2 * b + h, 35:36, :] = right[b : b + 1]

    for p in range(pairs):

        @pl.when(has_above)
        def _():
            rim_down(p).wait_recv()

        @pl.when(has_below)
        def _():
            rim_up(p).wait_recv()

        for k in range(2):
            b = 2 * p + k
            out_ref[2 * b, 38:40, :] = rim_in[0, p, 6:8, k * LANES : (k + 1) * LANES]
            out_ref[2 * b + 1, 32:34, :] = rim_in[1, p, 0:2, k * LANES : (k + 1) * LANES]

    def deal(offset):
        other, device = peer(offset)
        return pltpu.make_async_remote_copy(
            src_ref=out_ref.at[other], dst_ref=got_ref.at[mine], send_sem=deal_send.at[offset], recv_sem=deal_recv.at[offset], device_id=device, device_id_type=MESH
        )

    def start_deal(offset, carry):
        deal(offset).start()
        return carry

    def await_deal(offset, carry):
        deal(offset).wait_recv()
        return carry

    lax.fori_loop(1, sims, start_deal, 0)
    got_ref[mine] = out_ref[mine]
    for p in range(pairs):
        sent(last, 1, p)
        sent(last + 1, 0, p)

        @pl.when(has_above)
        def _():
            rim_up(p).wait_send()

        @pl.when(has_below)
        def _():
            rim_down(p).wait_send()

    line_ref[...] = jnp.zeros_like(line_ref)
    sums_ref[...] = jnp.zeros_like(sums_ref)
    lax.fori_loop(1, sims, await_deal, 0)

    for d in range(sims):
        s = peer(d)[0]
        own = got_ref[s, 34:36, :]
        partner = 2.0 * got_ref[one_ref[s], 34:36, :] - got_ref[two_ref[s], 34:36, :]
        for side in range(2):
            line_ref[side, d : d + 1, :] = own[side : side + 1]
            line_ref[2 + side, d : d + 1, :] = partner[side : side + 1]
    own_l, own_r, g_l, g_r = (line_ref[k].T for k in range(4))

    def col(x, k):
        return x[k * REACH : (k + 1) * REACH, :]

    flow_ref[0] = 0.5 * col(own_l, 1) * (col(g_l, 2) - col(g_l, 0))
    flow_ref[1] = 0.5 * col(own_r, 1) * (col(g_r, 2) - col(g_r, 0))
    flow_ref[2] = col(g_l, 1)
    flow_ref[3] = col(g_r, 1)
    lane = lax.broadcasted_iota(jnp.int32, (REACH, LANES), 1)
    first, final = lane == 0, lane == LANES - 1
    depth = REACH + 8
    row_spot = pl.ds(pl.multiple_of(half * REACH, REACH), REACH)
    col_spot = pl.ds(pl.multiple_of(lax.axis_index("chips") * LANES, LANES), LANES)

    def home(offset):
        return pltpu.make_async_remote_copy(
            src_ref=est_ref.at[offset],
            dst_ref=result_ref.at[row_spot, col_spot],
            send_sem=home_send.at[offset],
            recv_sem=home_recv.at[offset],
            device_id=peer(offset)[1],
            device_id_type=MESH,
        )

    for d in range(sims):
        s = peer(d)[0]
        f = got_ref[s]
        g = 2.0 * got_ref[one_ref[s]] - got_ref[two_ref[s]]
        p = f * (pltpu.roll(g, depth - 1, 0) - pltpu.roll(g, 1, 0))
        by_rows = (pltpu.roll(p, depth - 1, 0) - pltpu.roll(p, 1, 0))[:REACH]
        f, g = f[:REACH], g[:REACH]

        def vector(k):
            return jnp.broadcast_to(flow_ref[k, :, d : d + 1], (REACH, LANES))

        ahead = jnp.where(final, vector(3), pltpu.roll(g, LANES - 1, 1))
        behind = jnp.where(first, vector(2), pltpu.roll(g, 1, 1))
        q = 0.5 * f * (ahead - behind)
        ahead = jnp.where(final, vector(1), pltpu.roll(q, LANES - 1, 1))
        behind = jnp.where(first, vector(0), pltpu.roll(q, 1, 1))
        value = 0.25 * by_rows + 0.5 * (ahead - behind)
        if d == 0:
            result_ref[row_spot, col_spot] = value
        else:
            est_ref[d] = value
            home(d).start()
        for o in range(OWNERS):
            sums_ref[o] += jnp.where(owner_ref[s] == o, value, 0.0)
    for o in range(OWNERS):
        tally = jnp.int32(0)
        for s in range(sims):
            tally = tally + (owner_ref[s] == o).astype(jnp.int32)
        sums_ref[o] = sums_ref[o] / jnp.full((REACH, LANES), jnp.maximum(tally, 1).astype(F32))

    swap = pltpu.make_async_remote_copy(
        src_ref=sums_ref, dst_ref=other_ref, send_sem=mean_send, recv_sem=mean_recv, device_id={"core": 1 - half}, device_id_type=MESH
    )
    swap.start()
    wide = LANES // 2

    @pl.when(half == 0)
    def _():
        mean_ref[:, 0:REACH, :] = sums_ref[:, :, 0:wide]

    @pl.when(half == 1)
    def _():
        mean_ref[:, REACH : 2 * REACH, :] = sums_ref[:, :, wide:LANES]

    swap.wait_recv()

    @pl.when(half == 0)
    def _():
        mean_ref[:, REACH : 2 * REACH, :] = other_ref[:, :, 0:wide]

    @pl.when(half == 1)
    def _():
        mean_ref[:, 0:REACH, :] = other_ref[:, :, wide:LANES]

    def await_home(offset, carry):
        pltpu.make_async_remote_copy(
            src_ref=est_ref.at[offset],
            dst_ref=result_ref.at[0:REACH, 0:LANES],
            send_sem=home_send.at[offset],
            recv_sem=home_recv.at[offset],
            device_id=peer(offset)[1],
            device_id_type=MESH,
        ).wait_recv()
        return carry

    def finish_sends(offset, carry):
        deal(offset).wait_send()
        home(offset).wait_send()
        return carry

    lax.fori_loop(1, sims, await_home, 0)
    swap.wait_send()
    lax.fori_loop(1, sims, finish_sends, 0)


def body(maps, weight, beam, pair_one, pair_two, owner):
    rows, cols = weight.shape
    pairs = cols // WIDE
    sims = cols // LANES * 2
    vmem, smem = pl.BlockSpec(memory_space=pltpu.VMEM), pl.BlockSpec(memory_space=pltpu.SMEM)
    est, mean = pl.pallas_call(
        whole_kernel,
        out_shape=(jax.ShapeDtypeStruct((rows, cols), F32), jax.ShapeDtypeStruct((OWNERS, rows, LANES // 2), F32)),
        in_specs=[smem] * 3 + [vmem] * 3,
        out_specs=(vmem, vmem),
        scratch_shapes=[
            pltpu.VMEM((8, WINDOW), F32),
            pltpu.VMEM((rows, cols), F32),
            pltpu.VMEM((rows, cols), F32),
            pltpu.VMEM((2, pairs, rows, WIDE), F32),
            pltpu.VMEM((STEPS, pairs, REACH, WIDE), F32),
            pltpu.VMEM((STEPS, pairs, REACH, WIDE), F32),
            pltpu.VMEM((2, pairs, 8, WIDE), F32),
            pltpu.VMEM((2, WINDOW, WIDE), BF16),
            pltpu.VMEM((2, WINDOW, WIDE), BF16),
            pltpu.VMEM((2, rows, 6 * rows), BF16),
            pltpu.VMEM((pairs, rows, WINDOW), BF16),
            pltpu.VMEM((pairs, rows, WINDOW), BF16),
            pltpu.VMEM((pairs, 6 * rows, WIDE), BF16),
            pltpu.VMEM((4, cols // LANES, rows), F32),
            pltpu.VMEM((sims, REACH + 8, LANES), F32),
            pltpu.VMEM((sims, REACH + 8, LANES), F32),
            pltpu.VMEM((4, LANES, LANES), F32),
            pltpu.VMEM((4, REACH, LANES), F32),
            pltpu.VMEM((sims, REACH, LANES), F32),
            pltpu.VMEM((OWNERS, REACH, LANES), F32),
            pltpu.VMEM((OWNERS, REACH, LANES), F32),
            pltpu.SemaphoreType.DMA((2, STEPS, pairs)),
            pltpu.SemaphoreType.DMA((2, STEPS, pairs)),
            pltpu.SemaphoreType.DMA((2, pairs)),
            pltpu.SemaphoreType.DMA((2, pairs)),
            pltpu.SemaphoreType.DMA((sims,)),
            pltpu.SemaphoreType.DMA((sims,)),
            pltpu.SemaphoreType.DMA((sims,)),
            pltpu.SemaphoreType.DMA((sims,)),
            pltpu.SemaphoreType.DMA,
            pltpu.SemaphoreType.DMA,
        ],
        compiler_params=pltpu.CompilerParams(collective_id=0, has_side_effects=True),
    )(pair_one, pair_two, owner, maps[0], weight, beam.reshape(1, TAPS))
    return est[None], mean


def solution(mesh):
    split = Mesh(mesh.devices.reshape(16, 2, mesh.shape["rows"]), ("chips", "core", "rows"))
    sims = ("chips", "core")
    return jax.shard_map(
        body,
        mesh=split,
        in_specs=(P(sims, "rows", None), P("rows", None), P(), P(), P(), P()),
        out_specs=(P(sims, "rows", None), P(None, "rows", sims)),
        check_vma=False,
    )
```

```python
import jax
import jax.numpy as jnp
from jax import lax
from jax.experimental import pallas as pl
from jax.experimental.pallas import tpu as pltpu
from jax.sharding import Mesh
from jax.sharding import PartitionSpec as P

TAPS = 65
ITERS = 3
OWNERS = 8
STEPS = 2 * ITERS + 1
REACH = 32
LANES = 128
WIDE = 256
WINDOW = 512
ridge_term = 0.5
step_size = 0.6
F32 = jnp.float32
BF16 = jnp.bfloat16
MESH = pl.DeviceIdType.MESH
SLOTS = (1549942144, 1337883281)
ITEMS = (-1249954688, -332997999)


def looked_up(words, at):
    return jnp.right_shift(jnp.where(at < 8, words[0], words[1]), 4 * (at % 8)) & 15


def halves(x):
    high = x.astype(BF16)
    return high, (x - high.astype(F32)).astype(BF16)


def dot(a, b):
    return jnp.dot(a, b, preferred_element_type=F32)


def whole_kernel(one_ref, two_ref, owner_ref, maps_ref, weight_ref, beam_ref, result_ref, mean_ref, move_ref, moved_ref, taps_ref, f_ref, source_ref, h_ref, top_ref, bottom_ref, rim_in, across_h, across_l, down, x_h, x_l, ext_ref, edge_ref, out_ref, got_ref, line_ref, flow_ref, est_ref, sums_ref, other_ref, send_sem, recv_sem, rim_send, rim_recv, deal_send, deal_recv, home_send, home_recv, move_send, move_recv, mean_send, mean_recv):
    count = lax.axis_size("rows")
    me = lax.axis_index("rows")
    half = lax.axis_index("core")
    chip = lax.axis_index("chips")
    mine = 2 * chip + half
    sims = got_ref.shape[0]

    group, spot, ring = me // 4, me % 4, mine // 2 % 8

    def device_at(rows_at, sims_at):
        return {"rows": rows_at, "chips": sims_at // 2, "core": sims_at % 2}

    def holder(slab_at, sim):
        slot = looked_up(SLOTS, slab_at % 4 * 4 + sim // 16 * 2 + sim % 2)
        return 4 * (slab_at // 4) + slot // 4, slot // 2 % 2 * 16 + sim // 2 % 8 * 2 + slot % 2

    item = looked_up(ITEMS, 4 * spot + mine // 16 * 2 + half)
    slab = 4 * group + item // 4
    held = item // 2 % 2 * 16 + ring * 2 + item % 2
    above, below = device_at(*holder(slab - 1, held)), device_at(*holder(slab + 1, held))
    has_above, has_below = slab > 0, slab < count - 1
    target_rows, target_sims = holder(me, mine)
    target, origin = device_at(target_rows, target_sims), device_at(slab, held)
    moves = jnp.logical_or(target_rows != me, target_sims != mine)
    rows, cols = f_ref.shape
    blocks, pairs = cols // LANES, cols // WIDE

    barrier = pltpu.get_barrier_semaphore()

    @pl.when(has_above)
    def _():
        pl.semaphore_signal(barrier, inc=1, device_id=above, device_id_type=MESH)

    @pl.when(has_below)
    def _():
        pl.semaphore_signal(barrier, inc=1, device_id=below, device_id_type=MESH)

    @pl.when(moves)
    def _():
        pl.semaphore_signal(barrier, inc=1, device_id=origin, device_id_type=MESH)

    def peer(offset):
        other = lax.rem(mine + offset, sims)
        return other, device_at(me, other)

    def dealt(offset):
        other = lax.rem(held + offset, sims)
        own = jnp.logical_and(other == mine, slab == me)
        return other, device_at(slab, other), own

    def dealer(offset):
        other = lax.rem(mine + sims - offset, sims)
        rows_at, sims_at = holder(me, other)
        own = jnp.logical_and(rows_at == me, sims_at == mine)
        return device_at(rows_at, sims_at), own

    def greet(offset, carry):
        pl.semaphore_signal(barrier, inc=1, device_id=peer(offset)[1], device_id_type=MESH)
        return carry

    def greet_dealer(offset, carry):
        device, own = dealer(offset)

        @pl.when(jnp.logical_not(own))
        def _():
            pl.semaphore_signal(barrier, inc=1, device_id=device, device_id_type=MESH)

        return carry

    lax.fori_loop(1, sims, greet, 0)
    lax.fori_loop(0, sims, greet_dealer, 0)

    def number(x):
        return jnp.where(x, 1, 0)

    def put_away(pair):
        span = slice(pair * WIDE, (pair + 1) * WIDE)
        move_ref[0, pair] = weight_ref[:, span] * maps_ref[:, span]
        move_ref[1, pair] = weight_ref[:, span]

    for p in range(pairs):
        put_away(p)
    pl.semaphore_wait(barrier, 2 * sims - 1 + number(has_above) + number(has_below) + number(moves) - number(slab == me))

    def move(kind, pair):
        return pltpu.make_async_remote_copy(
            src_ref=move_ref.at[kind, pair], dst_ref=moved_ref.at[kind, pair], send_sem=move_send.at[kind, pair], recv_sem=move_recv.at[kind, pair], device_id=target, device_id_type=MESH
        )

    def send_off(kind, pair):
        @pl.when(moves)
        def _():
            move(kind, pair).start()

        @pl.when(jnp.logical_not(moves))
        def _():
            pltpu.make_async_copy(move_ref.at[kind, pair], moved_ref.at[kind, pair], move_recv.at[kind, pair]).start()

    for p in range(pairs):
        send_off(0, p)

    taps_ref[...] = jnp.zeros_like(taps_ref)
    taps_ref[0:1, :TAPS] = beam_ref[...]
    taps = taps_ref[0:1, :] / jnp.sum(taps_ref[0:1, :], axis=1, keepdims=True)
    taps_ref[0:1, :] = taps
    square = (LANES, LANES)
    turned = jnp.broadcast_to(taps[:, :LANES], square).T
    places = lax.broadcasted_iota(jnp.int32, square, 0) + lax.broadcasted_iota(jnp.int32, square, 1)
    taps_ref[1:2, :LANES] = jnp.sum(jnp.where(places == TAPS - 1, turned, 0.0), axis=0, keepdims=True)

    def tables(way):
        line = jnp.broadcast_to(taps_ref[1 - way : 2 - way, :], (WINDOW, WINDOW))
        table = pltpu.roll(line, WINDOW - 160, 1, stride=1, stride_axis=0)[:, :WIDE]
        high, low = halves(table)
        across_h[way] = high
        across_l[way] = low
        line = jnp.broadcast_to(taps_ref[way : way + 1, :LANES], (rows, LANES))
        inside = pltpu.roll(line, LANES - REACH, 1, stride=1, stride_axis=0)
        over = pltpu.roll(line, 64, 1, stride=1, stride_axis=0)
        under = pltpu.roll(line, 0, 1, stride=1, stride_axis=0)
        place = lax.broadcasted_iota(jnp.int32, (rows, LANES), 1)
        rim = jnp.where(place < 96, over, under)
        high, low = halves(inside[:, :64])
        rim_h, rim_l = halves(rim[:, 64:])
        down[way] = jnp.concatenate([high, low, high, rim_h, rim_l, rim_h], axis=1)

    nothing = jnp.zeros((rows, LANES), BF16)
    for ref in (x_h, x_l):
        ref[0, :, 0:LANES] = nothing
        ref[pairs - 1, :, 3 * LANES : 4 * LANES] = nothing

    tops = (192, 256, 320)
    bottoms = (224, 288, 352)
    empty = jnp.zeros((pairs, REACH, WIDE), BF16)

    @pl.when(jnp.logical_not(has_above))
    def _():
        for at in tops:
            ext_ref[:, at : at + REACH, :] = empty
        rim_in[0] = jnp.zeros_like(rim_in[0])

    @pl.when(jnp.logical_not(has_below))
    def _():
        for at in bottoms:
            ext_ref[:, at : at + REACH, :] = empty
        rim_in[1] = jnp.zeros_like(rim_in[1])

    def put(block, value):
        high, low = halves(value)
        for pair in range(pairs):
            place = block - 2 * pair + 1
            if 0 <= place < 4:
                x_h[pair, :, place * LANES : (place + 1) * LANES] = high
                x_l[pair, :, place * LANES : (place + 1) * LANES] = low

    def up_copy(step, parity, pair):
        return pltpu.make_async_remote_copy(
            src_ref=h_ref.at[parity, pair, 0:REACH],
            dst_ref=bottom_ref.at[step, pair],
            send_sem=send_sem.at[0, step, pair],
            recv_sem=recv_sem.at[1, step, pair],
            device_id=above,
            device_id_type=MESH,
        )

    def down_copy(step, parity, pair):
        return pltpu.make_async_remote_copy(
            src_ref=h_ref.at[parity, pair, REACH : 2 * REACH],
            dst_ref=top_ref.at[step, pair],
            send_sem=send_sem.at[1, step, pair],
            recv_sem=recv_sem.at[0, step, pair],
            device_id=below,
            device_id_type=MESH,
        )

    def sent(step, parity, pair):
        @pl.when(has_above)
        def _():
            up_copy(step, parity, pair).wait_send()

        @pl.when(has_below)
        def _():
            down_copy(step, parity, pair).wait_send()

    def across(step, parity, way, pair, waits=True):
        if waits:
            sent(step - 2, parity, pair)
        high, low = x_h[pair], x_l[pair]
        both = dot(jnp.concatenate([high, low], axis=0), across_h[way])
        value = both[:rows] + both[rows:] + dot(high, across_l[way])
        h_ref[parity, pair] = value

        @pl.when(has_above)
        def _():
            up_copy(step, parity, pair).start()

        @pl.when(has_below)
        def _():
            down_copy(step, parity, pair).start()

        high, low = halves(value)
        ext_ref[pair, 0:rows] = high
        ext_ref[pair, rows : 2 * rows] = high
        ext_ref[pair, 2 * rows : 3 * rows] = low

    def downward(step, parity, way, pair):
        @pl.when(has_above)
        def _():
            down_copy(step, parity, pair).wait_recv()
            high, low = halves(top_ref[step, pair])
            for at, part in zip(tops, (high, high, low)):
                ext_ref[pair, at : at + REACH] = part

        @pl.when(has_below)
        def _():
            up_copy(step, parity, pair).wait_recv()
            high, low = halves(bottom_ref[step, pair])
            for at, part in zip(bottoms, (high, high, low)):
                ext_ref[pair, at : at + REACH] = part

        return dot(down[way], ext_ref[pair])

    spans = [slice(b * LANES, (b + 1) * LANES) for b in range(blocks)]
    tables(1)
    for p in range(pairs):
        move(0, p).wait_recv()
        for k in range(2):
            put(2 * p + k, moved_ref[0, p, :, k * LANES : (k + 1) * LANES])
        if p > 0:
            across(0, 0, 1, p - 1, waits=False)
            send_off(1, p - 1)
    across(0, 0, 1, pairs - 1, waits=False)
    send_off(1, pairs - 1)
    tables(0)

    def sweep(step, parity, way, use, after, ready=None):
        for p in range(pairs):
            if ready is not None:
                ready(p)
            total = downward(step, parity, way, p)
            for k in range(2):
                use(2 * p + k, total[:, k * LANES : (k + 1) * LANES])
            if after is not None:
                if p > 0:
                    after(p - 1)
                if p == pairs - 1:
                    after(p)

    def begin(b, total):
        first = step_size * total
        source_ref[:, spans[b]] = first
        f_ref[:, spans[b]] = first
        put(b, first)

    def weigh(b, total):
        put(b, moved_ref[1, b // 2, :, b % 2 * LANES : (b % 2 + 1) * LANES] * total)

    def renew(b, total):
        value = (1.0 - step_size * ridge_term) * f_ref[:, spans[b]] + source_ref[:, spans[b]] - step_size * total
        f_ref[:, spans[b]] = value
        return value

    sweep(0, 0, 1, begin, lambda p: across(1, 1, 0, p, waits=False))

    def iteration(turn, carry):
        step = 2 * turn + 1

        def ready(p):
            @pl.when(turn == 0)
            def _():
                move(1, p).wait_recv()

        sweep(step, 1, 0, weigh, lambda p: across(step + 1, 0, 1, p), ready)
        sweep(step + 1, 0, 1, lambda b, total: put(b, renew(b, total)), lambda p: across(step + 2, 1, 0, p))
        return carry

    lax.fori_loop(0, ITERS - 1, iteration, 0)
    last = 2 * ITERS - 1
    sweep(last, 1, 0, weigh, lambda p: across(last + 1, 0, 1, p))

    def rim_up(pair):
        return pltpu.make_async_remote_copy(
            src_ref=f_ref.at[0:8, pair * WIDE : (pair + 1) * WIDE],
            dst_ref=rim_in.at[1, pair],
            send_sem=rim_send.at[0, pair],
            recv_sem=rim_recv.at[1, pair],
            device_id=above,
            device_id_type=MESH,
        )

    def rim_down(pair):
        return pltpu.make_async_remote_copy(
            src_ref=f_ref.at[rows - 8 : rows, pair * WIDE : (pair + 1) * WIDE],
            dst_ref=rim_in.at[0, pair],
            send_sem=rim_send.at[1, pair],
            recv_sem=rim_recv.at[0, pair],
            device_id=below,
            device_id_type=MESH,
        )

    def finish(b, total):
        value = renew(b, total)
        if b % 2 == 1:
            pair = b // 2

            @pl.when(has_above)
            def _():
                rim_up(pair).start()

            @pl.when(has_below)
            def _():
                rim_down(pair).start()

        for h in range(2):
            out_ref[2 * b + h, 0:REACH, :] = value[h * REACH : (h + 1) * REACH]
            out_ref[2 * b + h, 36:38, :] = jnp.zeros((2, LANES), F32)
        out_ref[2 * b, 32:34, :] = value[REACH : REACH + 2]
        out_ref[2 * b + 1, 38:40, :] = value[REACH - 2 : REACH]
        turned = value.T
        for k, lane in enumerate((0, 1, 126, 127)):
            edge_ref[k, b : b + 1, :] = turned[lane : lane + 1, :]

    sweep(last + 1, 0, 1, finish, None)

    zero, one, two, three = (edge_ref[k] for k in range(4))
    gap = jnp.zeros((1, rows), F32)
    before = [jnp.concatenate([gap, x[:-1]], axis=0) for x in (two, three)]
    after = [jnp.concatenate([x[1:], gap], axis=0) for x in (zero, one)]
    blank = jnp.zeros((blocks, REACH), F32)
    for h in range(2):
        part = slice(h * REACH, (h + 1) * REACH)
        left = jnp.concatenate([before[0][:, part], before[1][:, part], zero[:, part], blank], axis=1)
        right = jnp.concatenate([three[:, part], after[0][:, part], after[1][:, part], blank], axis=1)
        for b in range(blocks):
            out_ref[2 * b + h, 34:35, :] = left[b : b + 1]
            out_ref[2 * b + h, 35:36, :] = right[b : b + 1]

    for p in range(pairs):

        @pl.when(has_above)
        def _():
            rim_down(p).wait_recv()

        @pl.when(has_below)
        def _():
            rim_up(p).wait_recv()

        for k in range(2):
            b = 2 * p + k
            out_ref[2 * b, 38:40, :] = rim_in[0, p, 6:8, k * LANES : (k + 1) * LANES]
            out_ref[2 * b + 1, 32:34, :] = rim_in[1, p, 0:2, k * LANES : (k + 1) * LANES]

    def deal(offset):
        other, device, own = dealt(offset)
        return pltpu.make_async_remote_copy(
            src_ref=out_ref.at[other], dst_ref=got_ref.at[held], send_sem=deal_send.at[offset], recv_sem=deal_recv.at[offset], device_id=device, device_id_type=MESH
        )

    def start_deal(offset, carry):
        other, device, own = dealt(offset)

        @pl.when(jnp.logical_not(own))
        def _():
            deal(offset).start()

        @pl.when(own)
        def _():
            pltpu.make_async_copy(out_ref.at[other], got_ref.at[held], deal_recv.at[offset]).start()

        return carry

    def await_deal(offset, carry):
        deal(offset).wait_recv()
        return carry

    lax.fori_loop(0, sims, start_deal, 0)
    for p in range(pairs):
        sent(last, 1, p)
        sent(last + 1, 0, p)

        @pl.when(has_above)
        def _():
            rim_up(p).wait_send()

        @pl.when(has_below)
        def _():
            rim_down(p).wait_send()

    line_ref[...] = jnp.zeros_like(line_ref)
    sums_ref[...] = jnp.zeros_like(sums_ref)
    lax.fori_loop(0, sims, await_deal, 0)

    for d in range(sims):
        s = peer(d)[0]
        own = got_ref[s, 34:36, :]
        partner = 2.0 * got_ref[one_ref[s], 34:36, :] - got_ref[two_ref[s], 34:36, :]
        for side in range(2):
            line_ref[side, d : d + 1, :] = own[side : side + 1]
            line_ref[2 + side, d : d + 1, :] = partner[side : side + 1]
    own_l, own_r, g_l, g_r = (line_ref[k].T for k in range(4))

    def col(x, k):
        return x[k * REACH : (k + 1) * REACH, :]

    flow_ref[0] = 0.5 * col(own_l, 1) * (col(g_l, 2) - col(g_l, 0))
    flow_ref[1] = 0.5 * col(own_r, 1) * (col(g_r, 2) - col(g_r, 0))
    flow_ref[2] = col(g_l, 1)
    flow_ref[3] = col(g_r, 1)
    lane = lax.broadcasted_iota(jnp.int32, (REACH, LANES), 1)
    first, final = lane == 0, lane == LANES - 1
    depth = REACH + 8
    row_spot = pl.ds(pl.multiple_of(half * REACH, REACH), REACH)
    col_spot = pl.ds(pl.multiple_of(chip * LANES, LANES), LANES)

    def home(offset):
        return pltpu.make_async_remote_copy(
            src_ref=est_ref.at[offset],
            dst_ref=result_ref.at[row_spot, col_spot],
            send_sem=home_send.at[offset],
            recv_sem=home_recv.at[offset],
            device_id=peer(offset)[1],
            device_id_type=MESH,
        )

    for d in range(sims):
        s = peer(d)[0]
        f = got_ref[s]
        g = 2.0 * got_ref[one_ref[s]] - got_ref[two_ref[s]]
        p = f * (pltpu.roll(g, depth - 1, 0) - pltpu.roll(g, 1, 0))
        by_rows = (pltpu.roll(p, depth - 1, 0) - pltpu.roll(p, 1, 0))[:REACH]
        f, g = f[:REACH], g[:REACH]

        def vector(k):
            return jnp.broadcast_to(flow_ref[k, :, d : d + 1], (REACH, LANES))

        ahead = jnp.where(final, vector(3), pltpu.roll(g, LANES - 1, 1))
        behind = jnp.where(first, vector(2), pltpu.roll(g, 1, 1))
        q = 0.5 * f * (ahead - behind)
        ahead = jnp.where(final, vector(1), pltpu.roll(q, LANES - 1, 1))
        behind = jnp.where(first, vector(0), pltpu.roll(q, 1, 1))
        value = 0.25 * by_rows + 0.5 * (ahead - behind)
        if d == 0:
            result_ref[row_spot, col_spot] = value
        else:
            est_ref[d] = value
            home(d).start()
        for o in range(OWNERS):
            sums_ref[o] += jnp.where(owner_ref[s] == o, value, 0.0)
    for o in range(OWNERS):
        tally = jnp.int32(0)
        for s in range(sims):
            tally = tally + (owner_ref[s] == o).astype(jnp.int32)
        sums_ref[o] = sums_ref[o] / jnp.full((REACH, LANES), jnp.maximum(tally, 1).astype(F32))

    swap = pltpu.make_async_remote_copy(
        src_ref=sums_ref, dst_ref=other_ref, send_sem=mean_send, recv_sem=mean_recv, device_id=device_at(me, 2 * chip + 1 - half), device_id_type=MESH
    )
    swap.start()
    wide = LANES // 2

    @pl.when(half == 0)
    def _():
        mean_ref[:, 0:REACH, :] = sums_ref[:, :, 0:wide]

    @pl.when(half == 1)
    def _():
        mean_ref[:, REACH : 2 * REACH, :] = sums_ref[:, :, wide:LANES]

    swap.wait_recv()

    @pl.when(half == 0)
    def _():
        mean_ref[:, REACH : 2 * REACH, :] = other_ref[:, :, 0:wide]

    @pl.when(half == 1)
    def _():
        mean_ref[:, 0:REACH, :] = other_ref[:, :, wide:LANES]

    def await_home(offset, carry):
        pltpu.make_async_remote_copy(
            src_ref=est_ref.at[offset],
            dst_ref=result_ref.at[0:REACH, 0:LANES],
            send_sem=home_send.at[offset],
            recv_sem=home_recv.at[offset],
            device_id=peer(offset)[1],
            device_id_type=MESH,
        ).wait_recv()
        return carry

    def finish_homes(offset, carry):
        home(offset).wait_send()
        return carry

    def finish_deals(offset, carry):
        @pl.when(jnp.logical_not(dealt(offset)[2]))
        def _():
            deal(offset).wait_send()

        return carry

    lax.fori_loop(1, sims, await_home, 0)
    swap.wait_send()
    lax.fori_loop(1, sims, finish_homes, 0)
    lax.fori_loop(0, sims, finish_deals, 0)

    @pl.when(moves)
    def _():
        for kind in range(2):
            for p in range(pairs):
                move(kind, p).wait_send()


def body(maps, weight, beam, pair_one, pair_two, owner):
    rows, cols = weight.shape
    pairs = cols // WIDE
    sims = cols // LANES * 2
    vmem, smem = pl.BlockSpec(memory_space=pltpu.VMEM), pl.BlockSpec(memory_space=pltpu.SMEM)
    est, mean = pl.pallas_call(
        whole_kernel,
        out_shape=(jax.ShapeDtypeStruct((rows, cols), F32), jax.ShapeDtypeStruct((OWNERS, rows, LANES // 2), F32)),
        in_specs=[smem] * 3 + [vmem] * 3,
        out_specs=(vmem, vmem),
        scratch_shapes=[
            pltpu.VMEM((2, pairs, rows, WIDE), F32),
            pltpu.VMEM((2, pairs, rows, WIDE), F32),
            pltpu.VMEM((8, WINDOW), F32),
            pltpu.VMEM((rows, cols), F32),
            pltpu.VMEM((rows, cols), F32),
            pltpu.VMEM((2, pairs, rows, WIDE), F32),
            pltpu.VMEM((STEPS, pairs, REACH, WIDE), F32),
            pltpu.VMEM((STEPS, pairs, REACH, WIDE), F32),
            pltpu.VMEM((2, pairs, 8, WIDE), F32),
            pltpu.VMEM((2, WINDOW, WIDE), BF16),
            pltpu.VMEM((2, WINDOW, WIDE), BF16),
            pltpu.VMEM((2, rows, 6 * rows), BF16),
            pltpu.VMEM((pairs, rows, WINDOW), BF16),
            pltpu.VMEM((pairs, rows, WINDOW), BF16),
            pltpu.VMEM((pairs, 6 * rows, WIDE), BF16),
            pltpu.VMEM((4, cols // LANES, rows), F32),
            pltpu.VMEM((sims, REACH + 8, LANES), F32),
            pltpu.VMEM((sims, REACH + 8, LANES), F32),
            pltpu.VMEM((4, LANES, LANES), F32),
            pltpu.VMEM((4, REACH, LANES), F32),
            pltpu.VMEM((sims, REACH, LANES), F32),
            pltpu.VMEM((OWNERS, REACH, LANES), F32),
            pltpu.VMEM((OWNERS, REACH, LANES), F32),
            pltpu.SemaphoreType.DMA((2, STEPS, pairs)),
            pltpu.SemaphoreType.DMA((2, STEPS, pairs)),
            pltpu.SemaphoreType.DMA((2, pairs)),
            pltpu.SemaphoreType.DMA((2, pairs)),
            pltpu.SemaphoreType.DMA((sims,)),
            pltpu.SemaphoreType.DMA((sims,)),
            pltpu.SemaphoreType.DMA((sims,)),
            pltpu.SemaphoreType.DMA((sims,)),
            pltpu.SemaphoreType.DMA((2, pairs)),
            pltpu.SemaphoreType.DMA((2, pairs)),
            pltpu.SemaphoreType.DMA,
            pltpu.SemaphoreType.DMA,
        ],
        compiler_params=pltpu.CompilerParams(collective_id=0, has_side_effects=True),
    )(pair_one, pair_two, owner, maps[0], weight, beam.reshape(1, TAPS))
    return est[None], mean


def solution(mesh):
    split = Mesh(mesh.devices.reshape(16, 2, mesh.shape["rows"]), ("chips", "core", "rows"))
    sims = ("chips", "core")
    return jax.shard_map(
        body,
        mesh=split,
        in_specs=(P(sims, "rows", None), P("rows", None), P(), P(), P(), P()),
        out_specs=(P(sims, "rows", None), P(None, "rows", sims)),
        check_vma=False,
    )
```

```python
import jax
import jax.numpy as jnp
from jax import lax
from jax.experimental import pallas as pl
from jax.experimental.pallas import tpu as pltpu
from jax.sharding import Mesh
from jax.sharding import PartitionSpec as P

TAPS = 65
ITERS = 3
OWNERS = 8
STEPS = 2 * ITERS + 1
REACH = 32
LANES = 128
WIDE = 256
WINDOW = 512
ridge_term = 0.5
step_size = 0.6
F32 = jnp.float32
BF16 = jnp.bfloat16
MESH = pl.DeviceIdType.MESH
SLOTS = (1549942144, 1337883281)
ITEMS = (-1249954688, -332997999)


def looked_up(words, at):
    return jnp.right_shift(jnp.where(at < 8, words[0], words[1]), 4 * (at % 8)) & 15


def halves(x):
    high = x.astype(BF16)
    return high, (x - high.astype(F32)).astype(BF16)


def dot(a, b):
    return jnp.dot(a, b, preferred_element_type=F32)


def whole_kernel(one_ref, two_ref, owner_ref, maps_ref, weight_ref, beam_ref, result_ref, mean_ref, move_ref, moved_ref, taps_ref, f_ref, source_ref, h_ref, top_ref, bottom_ref, rim_in, across_h, across_l, down, x_h, x_l, ext_ref, edge_ref, out_ref, got_ref, line_ref, flow_ref, est_ref, sums_ref, other_ref, send_sem, recv_sem, rim_send, rim_recv, deal_send, deal_recv, home_send, home_recv, move_send, move_recv, mean_send, mean_recv):
    count = lax.axis_size("rows")
    me = lax.axis_index("rows")
    half = lax.axis_index("core")
    chip = lax.axis_index("chips")
    mine = 2 * chip + half
    sims = got_ref.shape[0]

    group, spot, ring = me // 4, me % 4, mine // 2 % 8

    def device_at(rows_at, sims_at):
        return {"rows": rows_at, "chips": sims_at // 2, "core": sims_at % 2}

    def holder(slab_at, sim):
        slot = looked_up(SLOTS, slab_at % 4 * 4 + sim // 16 * 2 + sim % 2)
        return 4 * (slab_at // 4) + slot // 4, slot // 2 % 2 * 16 + sim // 2 % 8 * 2 + slot % 2

    item = looked_up(ITEMS, 4 * spot + mine // 16 * 2 + half)
    slab = 4 * group + item // 4
    held = item // 2 % 2 * 16 + ring * 2 + item % 2
    above, below = device_at(*holder(slab - 1, held)), device_at(*holder(slab + 1, held))
    has_above, has_below = slab > 0, slab < count - 1
    target_rows, target_sims = holder(me, mine)
    target, origin = device_at(target_rows, target_sims), device_at(slab, held)
    moves = jnp.logical_or(target_rows != me, target_sims != mine)
    rows, cols = f_ref.shape
    blocks, pairs = cols // LANES, cols // WIDE

    barrier = pltpu.get_barrier_semaphore()

    @pl.when(has_above)
    def _():
        pl.semaphore_signal(barrier, inc=1, device_id=above, device_id_type=MESH)

    @pl.when(has_below)
    def _():
        pl.semaphore_signal(barrier, inc=1, device_id=below, device_id_type=MESH)

    @pl.when(moves)
    def _():
        pl.semaphore_signal(barrier, inc=1, device_id=origin, device_id_type=MESH)

    def peer(offset):
        other = lax.rem(mine + offset, sims)
        return other, device_at(me, other)

    def dealt(offset):
        other = lax.rem(held + offset, sims)
        own = jnp.logical_and(other == mine, slab == me)
        return other, device_at(slab, other), own

    def dealer(offset):
        other = lax.rem(mine + sims - offset, sims)
        rows_at, sims_at = holder(me, other)
        own = jnp.logical_and(rows_at == me, sims_at == mine)
        return device_at(rows_at, sims_at), own

    def greet(offset, carry):
        pl.semaphore_signal(barrier, inc=1, device_id=peer(offset)[1], device_id_type=MESH)
        return carry

    def greet_dealer(offset, carry):
        device, own = dealer(offset)

        @pl.when(jnp.logical_not(own))
        def _():
            pl.semaphore_signal(barrier, inc=1, device_id=device, device_id_type=MESH)

        return carry

    lax.fori_loop(1, sims, greet, 0)
    lax.fori_loop(0, sims, greet_dealer, 0)

    def number(x):
        return jnp.where(x, 1, 0)

    def put_away(pair):
        span = slice(pair * WIDE, (pair + 1) * WIDE)
        move_ref[0, pair] = weight_ref[:, span] * maps_ref[:, span]
        move_ref[1, pair] = weight_ref[:, span]

    for p in range(pairs):
        put_away(p)
    pl.semaphore_wait(barrier, 2 * sims - 1 + number(has_above) + number(has_below) + number(moves) - number(slab == me))

    def move(kind, pair):
        return pltpu.make_async_remote_copy(
            src_ref=move_ref.at[kind, pair], dst_ref=moved_ref.at[kind, pair], send_sem=move_send.at[kind, pair], recv_sem=move_recv.at[kind, pair], device_id=target, device_id_type=MESH
        )

    def send_off(kind, pair):
        @pl.when(moves)
        def _():
            move(kind, pair).start()

        @pl.when(jnp.logical_not(moves))
        def _():
            pltpu.make_async_copy(move_ref.at[kind, pair], moved_ref.at[kind, pair], move_recv.at[kind, pair]).start()

    for p in range(pairs):
        send_off(0, p)

    taps_ref[...] = jnp.zeros_like(taps_ref)
    taps_ref[0:1, :TAPS] = beam_ref[...]
    taps = taps_ref[0:1, :] / jnp.sum(taps_ref[0:1, :], axis=1, keepdims=True)
    taps_ref[0:1, :] = taps
    square = (LANES, LANES)
    turned = jnp.broadcast_to(taps[:, :LANES], square).T
    places = lax.broadcasted_iota(jnp.int32, square, 0) + lax.broadcasted_iota(jnp.int32, square, 1)
    taps_ref[1:2, :LANES] = jnp.sum(jnp.where(places == TAPS - 1, turned, 0.0), axis=0, keepdims=True)

    def tables(way):
        line = jnp.broadcast_to(taps_ref[1 - way : 2 - way, :], (WINDOW, WINDOW))
        table = pltpu.roll(line, WINDOW - 160, 1, stride=1, stride_axis=0)[:, :WIDE]
        high, low = halves(table)
        across_h[way] = high
        across_l[way] = low
        line = jnp.broadcast_to(taps_ref[way : way + 1, :LANES], (rows, LANES))
        inside = pltpu.roll(line, LANES - REACH, 1, stride=1, stride_axis=0)
        over = pltpu.roll(line, 64, 1, stride=1, stride_axis=0)
        under = pltpu.roll(line, 0, 1, stride=1, stride_axis=0)
        place = lax.broadcasted_iota(jnp.int32, (rows, LANES), 1)
        rim = jnp.where(place < 96, over, under)
        high, low = halves(inside[:, :64])
        rim_h, rim_l = halves(rim[:, 64:])
        down[way] = jnp.concatenate([high, low, high, rim_h, rim_l, rim_h], axis=1)

    nothing = jnp.zeros((rows, LANES), BF16)
    for ref in (x_h, x_l):
        ref[0, :, 0:LANES] = nothing
        ref[pairs - 1, :, 3 * LANES : 4 * LANES] = nothing

    tops = (192, 256, 320)
    bottoms = (224, 288, 352)
    empty = jnp.zeros((pairs, REACH, WIDE), BF16)

    @pl.when(jnp.logical_not(has_above))
    def _():
        for at in tops:
            ext_ref[:, at : at + REACH, :] = empty
        rim_in[0] = jnp.zeros_like(rim_in[0])

    @pl.when(jnp.logical_not(has_below))
    def _():
        for at in bottoms:
            ext_ref[:, at : at + REACH, :] = empty
        rim_in[1] = jnp.zeros_like(rim_in[1])

    def put(block, value):
        high, low = halves(value)
        for pair in range(pairs):
            place = block - 2 * pair + 1
            if 0 <= place < 4:
                x_h[pair, :, place * LANES : (place + 1) * LANES] = high
                x_l[pair, :, place * LANES : (place + 1) * LANES] = low

    def up_copy(step, parity, pair):
        return pltpu.make_async_remote_copy(
            src_ref=h_ref.at[parity, pair, 0:REACH],
            dst_ref=bottom_ref.at[step, pair],
            send_sem=send_sem.at[0, step, pair],
            recv_sem=recv_sem.at[1, step, pair],
            device_id=above,
            device_id_type=MESH,
        )

    def down_copy(step, parity, pair):
        return pltpu.make_async_remote_copy(
            src_ref=h_ref.at[parity, pair, REACH : 2 * REACH],
            dst_ref=top_ref.at[step, pair],
            send_sem=send_sem.at[1, step, pair],
            recv_sem=recv_sem.at[0, step, pair],
            device_id=below,
            device_id_type=MESH,
        )

    def sent(step, parity, pair):
        @pl.when(has_above)
        def _():
            up_copy(step, parity, pair).wait_send()

        @pl.when(has_below)
        def _():
            down_copy(step, parity, pair).wait_send()

    def across(step, parity, way, pair, waits=True):
        if waits:
            sent(step - 2, parity, pair)
        high, low = x_h[pair], x_l[pair]
        both = dot(jnp.concatenate([high, low], axis=0), across_h[way])
        value = both[:rows] + both[rows:] + dot(high, across_l[way])
        h_ref[parity, pair] = value

        @pl.when(has_above)
        def _():
            up_copy(step, parity, pair).start()

        @pl.when(has_below)
        def _():
            down_copy(step, parity, pair).start()

        high, low = halves(value)
        ext_ref[pair, 0:rows] = high
        ext_ref[pair, rows : 2 * rows] = high
        ext_ref[pair, 2 * rows : 3 * rows] = low

    def downward(step, parity, way, pair):
        @pl.when(has_above)
        def _():
            down_copy(step, parity, pair).wait_recv()
            high, low = halves(top_ref[step, pair])
            for at, part in zip(tops, (high, high, low)):
                ext_ref[pair, at : at + REACH] = part

        @pl.when(has_below)
        def _():
            up_copy(step, parity, pair).wait_recv()
            high, low = halves(bottom_ref[step, pair])
            for at, part in zip(bottoms, (high, high, low)):
                ext_ref[pair, at : at + REACH] = part

        return dot(down[way], ext_ref[pair])

    spans = [slice(b * LANES, (b + 1) * LANES) for b in range(blocks)]
    tables(1)
    for p in range(pairs):
        move(0, p).wait_recv()
        for k in range(2):
            put(2 * p + k, moved_ref[0, p, :, k * LANES : (k + 1) * LANES])
        if p > 0:
            across(0, 0, 1, p - 1, waits=False)
            send_off(1, p - 1)
    across(0, 0, 1, pairs - 1, waits=False)
    send_off(1, pairs - 1)
    tables(0)

    def sweep(step, parity, way, use, after, ready=None):
        for p in range(pairs):
            if ready is not None:
                ready(p)
            total = downward(step, parity, way, p)
            for k in range(2):
                use(2 * p + k, total[:, k * LANES : (k + 1) * LANES])
            if after is not None:
                if p > 0:
                    after(p - 1)
                if p == pairs - 1:
                    after(p)

    def begin(b, total):
        first = step_size * total
        source_ref[:, spans[b]] = first
        f_ref[:, spans[b]] = first
        put(b, first)

    def weigh(b, total):
        put(b, moved_ref[1, b // 2, :, b % 2 * LANES : (b % 2 + 1) * LANES] * total)

    def renew(b, total):
        value = (1.0 - step_size * ridge_term) * f_ref[:, spans[b]] + source_ref[:, spans[b]] - step_size * total
        f_ref[:, spans[b]] = value
        return value

    sweep(0, 0, 1, begin, lambda p: across(1, 1, 0, p, waits=False))

    def iteration(turn, carry):
        step = 2 * turn + 1

        def ready(p):
            @pl.when(turn == 0)
            def _():
                move(1, p).wait_recv()

        sweep(step, 1, 0, weigh, lambda p: across(step + 1, 0, 1, p), ready)
        sweep(step + 1, 0, 1, lambda b, total: put(b, renew(b, total)), lambda p: across(step + 2, 1, 0, p))
        return carry

    lax.fori_loop(0, ITERS - 1, iteration, 0)
    last = 2 * ITERS - 1
    sweep(last, 1, 0, weigh, lambda p: across(last + 1, 0, 1, p))

    def rim_up(pair):
        return pltpu.make_async_remote_copy(
            src_ref=f_ref.at[0:8, pair * WIDE : (pair + 1) * WIDE],
            dst_ref=rim_in.at[1, pair],
            send_sem=rim_send.at[0, pair],
            recv_sem=rim_recv.at[1, pair],
            device_id=above,
            device_id_type=MESH,
        )

    def rim_down(pair):
        return pltpu.make_async_remote_copy(
            src_ref=f_ref.at[rows - 8 : rows, pair * WIDE : (pair + 1) * WIDE],
            dst_ref=rim_in.at[0, pair],
            send_sem=rim_send.at[1, pair],
            recv_sem=rim_recv.at[0, pair],
            device_id=below,
            device_id_type=MESH,
        )

    def finish(b, total):
        value = renew(b, total)
        if b % 2 == 1:
            pair = b // 2

            @pl.when(has_above)
            def _():
                rim_up(pair).start()

            @pl.when(has_below)
            def _():
                rim_down(pair).start()

        for h in range(2):
            out_ref[2 * b + h, 0:REACH, :] = value[h * REACH : (h + 1) * REACH]
            out_ref[2 * b + h, 36:38, :] = jnp.zeros((2, LANES), F32)
        out_ref[2 * b, 32:34, :] = value[REACH : REACH + 2]
        out_ref[2 * b + 1, 38:40, :] = value[REACH - 2 : REACH]
        turned = value.T
        for k, lane in enumerate((0, 1, 126, 127)):
            edge_ref[k, b : b + 1, :] = turned[lane : lane + 1, :]

    sweep(last + 1, 0, 1, finish, None)

    def deal(kind, offset):
        other, device, own = dealt(offset)
        part = slice(0, REACH) if kind == 0 else slice(REACH, REACH + 8)
        return pltpu.make_async_remote_copy(
            src_ref=out_ref.at[other, part],
            dst_ref=got_ref.at[held, part],
            send_sem=deal_send.at[kind, offset],
            recv_sem=deal_recv.at[kind, offset],
            device_id=device,
            device_id_type=MESH,
        )

    def start_deals(kind):
        part = slice(0, REACH) if kind == 0 else slice(REACH, REACH + 8)

        def start_deal(offset, carry):
            other, device, own = dealt(offset)

            @pl.when(jnp.logical_not(own))
            def _():
                deal(kind, offset).start()

            @pl.when(own)
            def _():
                pltpu.make_async_copy(out_ref.at[other, part], got_ref.at[held, part], deal_recv.at[kind, offset]).start()

            return carry

        lax.fori_loop(0, sims, start_deal, 0)

    def await_deal(offset, carry):
        for kind in range(2):
            deal(kind, offset).wait_recv()
        return carry

    start_deals(0)

    zero, one, two, three = (edge_ref[k] for k in range(4))
    gap = jnp.zeros((1, rows), F32)
    before = [jnp.concatenate([gap, x[:-1]], axis=0) for x in (two, three)]
    after = [jnp.concatenate([x[1:], gap], axis=0) for x in (zero, one)]
    blank = jnp.zeros((blocks, REACH), F32)
    for h in range(2):
        part = slice(h * REACH, (h + 1) * REACH)
        left = jnp.concatenate([before[0][:, part], before[1][:, part], zero[:, part], blank], axis=1)
        right = jnp.concatenate([three[:, part], after[0][:, part], after[1][:, part], blank], axis=1)
        for b in range(blocks):
            out_ref[2 * b + h, 34:35, :] = left[b : b + 1]
            out_ref[2 * b + h, 35:36, :] = right[b : b + 1]

    for p in range(pairs):

        @pl.when(has_above)
        def _():
            rim_down(p).wait_recv()

        @pl.when(has_below)
        def _():
            rim_up(p).wait_recv()

        for k in range(2):
            b = 2 * p + k
            out_ref[2 * b, 38:40, :] = rim_in[0, p, 6:8, k * LANES : (k + 1) * LANES]
            out_ref[2 * b + 1, 32:34, :] = rim_in[1, p, 0:2, k * LANES : (k + 1) * LANES]

    start_deals(1)
    for p in range(pairs):
        sent(last, 1, p)
        sent(last + 1, 0, p)

        @pl.when(has_above)
        def _():
            rim_up(p).wait_send()

        @pl.when(has_below)
        def _():
            rim_down(p).wait_send()

    line_ref[...] = jnp.zeros_like(line_ref)
    sums_ref[...] = jnp.zeros_like(sums_ref)
    lax.fori_loop(0, sims, await_deal, 0)

    for d in range(sims):
        s = peer(d)[0]
        own = got_ref[s, 34:36, :]
        partner = 2.0 * got_ref[one_ref[s], 34:36, :] - got_ref[two_ref[s], 34:36, :]
        for side in range(2):
            line_ref[side, d : d + 1, :] = own[side : side + 1]
            line_ref[2 + side, d : d + 1, :] = partner[side : side + 1]
    own_l, own_r, g_l, g_r = (line_ref[k].T for k in range(4))

    def col(x, k):
        return x[k * REACH : (k + 1) * REACH, :]

    flow_ref[0] = 0.5 * col(own_l, 1) * (col(g_l, 2) - col(g_l, 0))
    flow_ref[1] = 0.5 * col(own_r, 1) * (col(g_r, 2) - col(g_r, 0))
    flow_ref[2] = col(g_l, 1)
    flow_ref[3] = col(g_r, 1)
    lane = lax.broadcasted_iota(jnp.int32, (REACH, LANES), 1)
    first, final = lane == 0, lane == LANES - 1
    depth = REACH + 8
    row_spot = pl.ds(pl.multiple_of(half * REACH, REACH), REACH)
    col_spot = pl.ds(pl.multiple_of(chip * LANES, LANES), LANES)

    def home(offset):
        return pltpu.make_async_remote_copy(
            src_ref=est_ref.at[offset],
            dst_ref=result_ref.at[row_spot, col_spot],
            send_sem=home_send.at[offset],
            recv_sem=home_recv.at[offset],
            device_id=peer(offset)[1],
            device_id_type=MESH,
        )

    for d in range(sims):
        s = peer(d)[0]
        f = got_ref[s]
        g = 2.0 * got_ref[one_ref[s]] - got_ref[two_ref[s]]
        p = f * (pltpu.roll(g, depth - 1, 0) - pltpu.roll(g, 1, 0))
        by_rows = (pltpu.roll(p, depth - 1, 0) - pltpu.roll(p, 1, 0))[:REACH]
        f, g = f[:REACH], g[:REACH]

        def vector(k):
            return jnp.broadcast_to(flow_ref[k, :, d : d + 1], (REACH, LANES))

        ahead = jnp.where(final, vector(3), pltpu.roll(g, LANES - 1, 1))
        behind = jnp.where(first, vector(2), pltpu.roll(g, 1, 1))
        q = 0.5 * f * (ahead - behind)
        ahead = jnp.where(final, vector(1), pltpu.roll(q, LANES - 1, 1))
        behind = jnp.where(first, vector(0), pltpu.roll(q, 1, 1))
        value = 0.25 * by_rows + 0.5 * (ahead - behind)
        if d == 0:
            result_ref[row_spot, col_spot] = value
        else:
            est_ref[d] = value
            home(d).start()
        for o in range(OWNERS):
            sums_ref[o] += jnp.where(owner_ref[s] == o, value, 0.0)
    for o in range(OWNERS):
        tally = jnp.int32(0)
        for s in range(sims):
            tally = tally + (owner_ref[s] == o).astype(jnp.int32)
        sums_ref[o] = sums_ref[o] / jnp.full((REACH, LANES), jnp.maximum(tally, 1).astype(F32))

    swap = pltpu.make_async_remote_copy(
        src_ref=sums_ref, dst_ref=other_ref, send_sem=mean_send, recv_sem=mean_recv, device_id=device_at(me, 2 * chip + 1 - half), device_id_type=MESH
    )
    swap.start()
    wide = LANES // 2

    @pl.when(half == 0)
    def _():
        mean_ref[:, 0:REACH, :] = sums_ref[:, :, 0:wide]

    @pl.when(half == 1)
    def _():
        mean_ref[:, REACH : 2 * REACH, :] = sums_ref[:, :, wide:LANES]

    swap.wait_recv()

    @pl.when(half == 0)
    def _():
        mean_ref[:, REACH : 2 * REACH, :] = other_ref[:, :, 0:wide]

    @pl.when(half == 1)
    def _():
        mean_ref[:, 0:REACH, :] = other_ref[:, :, wide:LANES]

    def await_home(offset, carry):
        pltpu.make_async_remote_copy(
            src_ref=est_ref.at[offset],
            dst_ref=result_ref.at[0:REACH, 0:LANES],
            send_sem=home_send.at[offset],
            recv_sem=home_recv.at[offset],
            device_id=peer(offset)[1],
            device_id_type=MESH,
        ).wait_recv()
        return carry

    def finish_homes(offset, carry):
        home(offset).wait_send()
        return carry

    def finish_deals(offset, carry):
        @pl.when(jnp.logical_not(dealt(offset)[2]))
        def _():
            for kind in range(2):
                deal(kind, offset).wait_send()

        return carry

    lax.fori_loop(1, sims, await_home, 0)
    swap.wait_send()
    lax.fori_loop(1, sims, finish_homes, 0)
    lax.fori_loop(0, sims, finish_deals, 0)

    @pl.when(moves)
    def _():
        for kind in range(2):
            for p in range(pairs):
                move(kind, p).wait_send()


def body(maps, weight, beam, pair_one, pair_two, owner):
    rows, cols = weight.shape
    pairs = cols // WIDE
    sims = cols // LANES * 2
    vmem, smem = pl.BlockSpec(memory_space=pltpu.VMEM), pl.BlockSpec(memory_space=pltpu.SMEM)
    est, mean = pl.pallas_call(
        whole_kernel,
        out_shape=(jax.ShapeDtypeStruct((rows, cols), F32), jax.ShapeDtypeStruct((OWNERS, rows, LANES // 2), F32)),
        in_specs=[smem] * 3 + [vmem] * 3,
        out_specs=(vmem, vmem),
        scratch_shapes=[
            pltpu.VMEM((2, pairs, rows, WIDE), F32),
            pltpu.VMEM((2, pairs, rows, WIDE), F32),
            pltpu.VMEM((8, WINDOW), F32),
            pltpu.VMEM((rows, cols), F32),
            pltpu.VMEM((rows, cols), F32),
            pltpu.VMEM((2, pairs, rows, WIDE), F32),
            pltpu.VMEM((STEPS, pairs, REACH, WIDE), F32),
            pltpu.VMEM((STEPS, pairs, REACH, WIDE), F32),
            pltpu.VMEM((2, pairs, 8, WIDE), F32),
            pltpu.VMEM((2, WINDOW, WIDE), BF16),
            pltpu.VMEM((2, WINDOW, WIDE), BF16),
            pltpu.VMEM((2, rows, 6 * rows), BF16),
            pltpu.VMEM((pairs, rows, WINDOW), BF16),
            pltpu.VMEM((pairs, rows, WINDOW), BF16),
            pltpu.VMEM((pairs, 6 * rows, WIDE), BF16),
            pltpu.VMEM((4, cols // LANES, rows), F32),
            pltpu.VMEM((sims, REACH + 8, LANES), F32),
            pltpu.VMEM((sims, REACH + 8, LANES), F32),
            pltpu.VMEM((4, LANES, LANES), F32),
            pltpu.VMEM((4, REACH, LANES), F32),
            pltpu.VMEM((sims, REACH, LANES), F32),
            pltpu.VMEM((OWNERS, REACH, LANES), F32),
            pltpu.VMEM((OWNERS, REACH, LANES), F32),
            pltpu.SemaphoreType.DMA((2, STEPS, pairs)),
            pltpu.SemaphoreType.DMA((2, STEPS, pairs)),
            pltpu.SemaphoreType.DMA((2, pairs)),
            pltpu.SemaphoreType.DMA((2, pairs)),
            pltpu.SemaphoreType.DMA((2, sims)),
            pltpu.SemaphoreType.DMA((2, sims)),
            pltpu.SemaphoreType.DMA((sims,)),
            pltpu.SemaphoreType.DMA((sims,)),
            pltpu.SemaphoreType.DMA((2, pairs)),
            pltpu.SemaphoreType.DMA((2, pairs)),
            pltpu.SemaphoreType.DMA,
            pltpu.SemaphoreType.DMA,
        ],
        compiler_params=pltpu.CompilerParams(collective_id=0, has_side_effects=True),
    )(pair_one, pair_two, owner, maps[0], weight, beam.reshape(1, TAPS))
    return est[None], mean


def solution(mesh):
    split = Mesh(mesh.devices.reshape(16, 2, mesh.shape["rows"]), ("chips", "core", "rows"))
    sims = ("chips", "core")
    return jax.shard_map(
        body,
        mesh=split,
        in_specs=(P(sims, "rows", None), P("rows", None), P(), P(), P(), P()),
        out_specs=(P(sims, "rows", None), P(None, "rows", sims)),
        check_vma=False,
    )
```

```python
import jax
import jax.numpy as jnp
from jax import lax
from jax.experimental import pallas as pl
from jax.experimental.pallas import tpu as pltpu
from jax.sharding import Mesh
from jax.sharding import PartitionSpec as P

TAPS = 65
ITERS = 3
OWNERS = 8
STEPS = 2 * ITERS + 1
REACH = 32
LANES = 128
WIDE = 256
WINDOW = 512
ridge_term = 0.5
step_size = 0.6
F32 = jnp.float32
BF16 = jnp.bfloat16
MESH = pl.DeviceIdType.MESH
SLOTS = (1549942144, 1337883281)
ITEMS = (-1249954688, -332997999)


def looked_up(words, at):
    return jnp.right_shift(jnp.where(at < 8, words[0], words[1]), 4 * (at % 8)) & 15


def halves(x):
    high = x.astype(BF16)
    return high, (x - high.astype(F32)).astype(BF16)


def dot(a, b):
    return jnp.dot(a, b, preferred_element_type=F32)


def whole_kernel(one_ref, two_ref, owner_ref, maps_ref, weight_ref, beam_ref, result_ref, mean_ref, move_ref, moved_ref, taps_ref, f_ref, source_ref, h_ref, top_ref, bottom_ref, rim_in, across_h, across_l, down, x_h, x_l, ext_ref, edge_ref, out_ref, got_ref, line_ref, flow_ref, est_ref, sums_ref, other_ref, send_sem, recv_sem, rim_send, rim_recv, deal_send, deal_recv, home_send, home_recv, move_send, move_recv, mean_send, mean_recv):
    count = lax.axis_size("rows")
    me = lax.axis_index("rows")
    half = lax.axis_index("core")
    chip = lax.axis_index("chips")
    mine = 2 * chip + half
    sims = got_ref.shape[0]

    group, spot, ring = me // 4, me % 4, mine // 2 % 8

    def device_at(rows_at, sims_at):
        return {"rows": rows_at, "chips": sims_at // 2, "core": sims_at % 2}

    def holder(slab_at, sim):
        slot = looked_up(SLOTS, slab_at % 4 * 4 + sim // 16 * 2 + sim % 2)
        return 4 * (slab_at // 4) + slot // 4, slot // 2 % 2 * 16 + sim // 2 % 8 * 2 + slot % 2

    item = looked_up(ITEMS, 4 * spot + mine // 16 * 2 + half)
    slab = 4 * group + item // 4
    held = item // 2 % 2 * 16 + ring * 2 + item % 2
    above, below = device_at(*holder(slab - 1, held)), device_at(*holder(slab + 1, held))
    has_above, has_below = slab > 0, slab < count - 1
    target_rows, target_sims = holder(me, mine)
    target, origin = device_at(target_rows, target_sims), device_at(slab, held)
    moves = jnp.logical_or(target_rows != me, target_sims != mine)
    rows, cols = f_ref.shape
    blocks, pairs = cols // LANES, cols // WIDE

    barrier = pltpu.get_barrier_semaphore()

    @pl.when(has_above)
    def _():
        pl.semaphore_signal(barrier, inc=1, device_id=above, device_id_type=MESH)

    @pl.when(has_below)
    def _():
        pl.semaphore_signal(barrier, inc=1, device_id=below, device_id_type=MESH)

    @pl.when(moves)
    def _():
        pl.semaphore_signal(barrier, inc=1, device_id=origin, device_id_type=MESH)

    def peer(offset):
        other = lax.rem(mine + offset, sims)
        return other, device_at(me, other)

    def dealt(offset):
        other = lax.rem(held + offset, sims)
        own = jnp.logical_and(other == mine, slab == me)
        return other, device_at(slab, other), own

    def dealer(offset):
        other = lax.rem(mine + sims - offset, sims)
        rows_at, sims_at = holder(me, other)
        own = jnp.logical_and(rows_at == me, sims_at == mine)
        return device_at(rows_at, sims_at), own

    def greet(offset, carry):
        pl.semaphore_signal(barrier, inc=1, device_id=peer(offset)[1], device_id_type=MESH)
        return carry

    def greet_dealer(offset, carry):
        device, own = dealer(offset)

        @pl.when(jnp.logical_not(own))
        def _():
            pl.semaphore_signal(barrier, inc=1, device_id=device, device_id_type=MESH)

        return carry

    lax.fori_loop(1, sims, greet, 0)
    lax.fori_loop(0, sims, greet_dealer, 0)

    def number(x):
        return jnp.where(x, 1, 0)

    def put_away(pair):
        span = slice(pair * WIDE, (pair + 1) * WIDE)
        move_ref[0, pair] = weight_ref[:, span] * maps_ref[:, span]
        move_ref[1, pair] = weight_ref[:, span]

    for p in range(pairs):
        put_away(p)
    pl.semaphore_wait(barrier, 2 * sims - 1 + number(has_above) + number(has_below) + number(moves) - number(slab == me))

    def move(kind, pair):
        return pltpu.make_async_remote_copy(
            src_ref=move_ref.at[kind, pair], dst_ref=moved_ref.at[kind, pair], send_sem=move_send.at[kind, pair], recv_sem=move_recv.at[kind, pair], device_id=target, device_id_type=MESH
        )

    def send_off(kind, pair):
        @pl.when(moves)
        def _():
            move(kind, pair).start()

        @pl.when(jnp.logical_not(moves))
        def _():
            pltpu.make_async_copy(move_ref.at[kind, pair], moved_ref.at[kind, pair], move_recv.at[kind, pair]).start()

    for p in range(pairs):
        send_off(0, p)

    taps_ref[...] = jnp.zeros_like(taps_ref)
    taps_ref[0:1, :TAPS] = beam_ref[...]
    taps = taps_ref[0:1, :] / jnp.sum(taps_ref[0:1, :], axis=1, keepdims=True)
    taps_ref[0:1, :] = taps
    square = (LANES, LANES)
    turned = jnp.broadcast_to(taps[:, :LANES], square).T
    places = lax.broadcasted_iota(jnp.int32, square, 0) + lax.broadcasted_iota(jnp.int32, square, 1)
    taps_ref[1:2, :LANES] = jnp.sum(jnp.where(places == TAPS - 1, turned, 0.0), axis=0, keepdims=True)

    def tables(way):
        line = jnp.broadcast_to(taps_ref[1 - way : 2 - way, :], (WINDOW, WINDOW))
        table = pltpu.roll(line, WINDOW - 160, 1, stride=1, stride_axis=0)[:, :WIDE]
        high, low = halves(table)
        across_h[way] = high
        across_l[way] = low
        line = jnp.broadcast_to(taps_ref[way : way + 1, :LANES], (rows, LANES))
        inside = pltpu.roll(line, LANES - REACH, 1, stride=1, stride_axis=0)
        over = pltpu.roll(line, 64, 1, stride=1, stride_axis=0)
        under = pltpu.roll(line, 0, 1, stride=1, stride_axis=0)
        place = lax.broadcasted_iota(jnp.int32, (rows, LANES), 1)
        rim = jnp.where(place < 96, over, under)
        high, low = halves(inside[:, :64])
        rim_h, rim_l = halves(rim[:, 64:])
        down[way] = jnp.concatenate([high, low, high, rim_h, rim_l, rim_h], axis=1)

    nothing = jnp.zeros((rows, LANES), BF16)
    for ref in (x_h, x_l):
        ref[0, :, 0:LANES] = nothing
        ref[pairs - 1, :, 3 * LANES : 4 * LANES] = nothing

    tops = (192, 256, 320)
    bottoms = (224, 288, 352)
    empty = jnp.zeros((pairs, REACH, WIDE), BF16)

    @pl.when(jnp.logical_not(has_above))
    def _():
        for at in tops:
            ext_ref[:, at : at + REACH, :] = empty
        rim_in[0] = jnp.zeros_like(rim_in[0])

    @pl.when(jnp.logical_not(has_below))
    def _():
        for at in bottoms:
            ext_ref[:, at : at + REACH, :] = empty
        rim_in[1] = jnp.zeros_like(rim_in[1])

    def put(block, value):
        high, low = halves(value)
        for pair in range(pairs):
            place = block - 2 * pair + 1
            if 0 <= place < 4:
                x_h[pair, :, place * LANES : (place + 1) * LANES] = high
                x_l[pair, :, place * LANES : (place + 1) * LANES] = low

    def up_copy(step, parity, pair):
        return pltpu.make_async_remote_copy(
            src_ref=h_ref.at[parity, pair, 0:REACH],
            dst_ref=bottom_ref.at[step, pair],
            send_sem=send_sem.at[0, step, pair],
            recv_sem=recv_sem.at[1, step, pair],
            device_id=above,
            device_id_type=MESH,
        )

    def down_copy(step, parity, pair):
        return pltpu.make_async_remote_copy(
            src_ref=h_ref.at[parity, pair, REACH : 2 * REACH],
            dst_ref=top_ref.at[step, pair],
            send_sem=send_sem.at[1, step, pair],
            recv_sem=recv_sem.at[0, step, pair],
            device_id=below,
            device_id_type=MESH,
        )

    def sent(step, parity, pair):
        @pl.when(has_above)
        def _():
            up_copy(step, parity, pair).wait_send()

        @pl.when(has_below)
        def _():
            down_copy(step, parity, pair).wait_send()

    def across(step, parity, way, pair, waits=True):
        if waits:
            sent(step - 2, parity, pair)
        high, low = x_h[pair], x_l[pair]
        both = dot(jnp.concatenate([high, low], axis=0), across_h[way])
        value = both[:rows] + both[rows:] + dot(high, across_l[way])
        h_ref[parity, pair] = value

        @pl.when(has_above)
        def _():
            up_copy(step, parity, pair).start()

        @pl.when(has_below)
        def _():
            down_copy(step, parity, pair).start()

        high, low = halves(value)
        ext_ref[pair, 0:rows] = high
        ext_ref[pair, rows : 2 * rows] = high
        ext_ref[pair, 2 * rows : 3 * rows] = low

    def downward(step, parity, way, pair):
        @pl.when(has_above)
        def _():
            down_copy(step, parity, pair).wait_recv()
            high, low = halves(top_ref[step, pair])
            for at, part in zip(tops, (high, high, low)):
                ext_ref[pair, at : at + REACH] = part

        @pl.when(has_below)
        def _():
            up_copy(step, parity, pair).wait_recv()
            high, low = halves(bottom_ref[step, pair])
            for at, part in zip(bottoms, (high, high, low)):
                ext_ref[pair, at : at + REACH] = part

        return dot(down[way], ext_ref[pair])

    spans = [slice(b * LANES, (b + 1) * LANES) for b in range(blocks)]
    tables(1)
    for p in range(pairs):
        move(0, p).wait_recv()
        for k in range(2):
            put(2 * p + k, moved_ref[0, p, :, k * LANES : (k + 1) * LANES])
        if p > 0:
            across(0, 0, 1, p - 1, waits=False)
            send_off(1, p - 1)
    across(0, 0, 1, pairs - 1, waits=False)
    send_off(1, pairs - 1)
    tables(0)

    def sweep(step, parity, way, use, after, ready=None):
        for p in range(pairs):
            if ready is not None:
                ready(p)
            total = downward(step, parity, way, p)
            for k in range(2):
                use(2 * p + k, total[:, k * LANES : (k + 1) * LANES])
            if after is not None:
                if p > 0:
                    after(p - 1)
                if p == pairs - 1:
                    after(p)

    def begin(b, total):
        first = step_size * total
        source_ref[:, spans[b]] = first
        f_ref[:, spans[b]] = first
        put(b, first)

    def weigh(b, total):
        put(b, moved_ref[1, b // 2, :, b % 2 * LANES : (b % 2 + 1) * LANES] * total)

    def renew(b, total):
        value = (1.0 - step_size * ridge_term) * f_ref[:, spans[b]] + source_ref[:, spans[b]] - step_size * total
        f_ref[:, spans[b]] = value
        return value

    sweep(0, 0, 1, begin, lambda p: across(1, 1, 0, p, waits=False))

    def iteration(turn, carry):
        step = 2 * turn + 1

        def ready(p):
            @pl.when(turn == 0)
            def _():
                move(1, p).wait_recv()

        sweep(step, 1, 0, weigh, lambda p: across(step + 1, 0, 1, p), ready)
        sweep(step + 1, 0, 1, lambda b, total: put(b, renew(b, total)), lambda p: across(step + 2, 1, 0, p))
        return carry

    lax.fori_loop(0, ITERS - 1, iteration, 0)
    last = 2 * ITERS - 1
    sweep(last, 1, 0, weigh, lambda p: across(last + 1, 0, 1, p))

    def rim_up(pair):
        return pltpu.make_async_remote_copy(
            src_ref=f_ref.at[0:8, pair * WIDE : (pair + 1) * WIDE],
            dst_ref=rim_in.at[1, pair],
            send_sem=rim_send.at[0, pair],
            recv_sem=rim_recv.at[1, pair],
            device_id=above,
            device_id_type=MESH,
        )

    def rim_down(pair):
        return pltpu.make_async_remote_copy(
            src_ref=f_ref.at[rows - 8 : rows, pair * WIDE : (pair + 1) * WIDE],
            dst_ref=rim_in.at[0, pair],
            send_sem=rim_send.at[1, pair],
            recv_sem=rim_recv.at[0, pair],
            device_id=below,
            device_id_type=MESH,
        )

    def finish(b, total):
        value = renew(b, total)
        if b % 2 == 1:
            pair = b // 2

            @pl.when(has_above)
            def _():
                rim_up(pair).start()

            @pl.when(has_below)
            def _():
                rim_down(pair).start()

        for h in range(2):
            out_ref[2 * b + h, 0:REACH, :] = value[h * REACH : (h + 1) * REACH]
            out_ref[2 * b + h, 36:38, :] = jnp.zeros((2, LANES), F32)
        out_ref[2 * b, 32:34, :] = value[REACH : REACH + 2]
        out_ref[2 * b + 1, 38:40, :] = value[REACH - 2 : REACH]
        turned = value.T
        for k, lane in enumerate((0, 1, 126, 127)):
            edge_ref[k, b : b + 1, :] = turned[lane : lane + 1, :]

    sweep(last + 1, 0, 1, finish, None)

    zero, one, two, three = (edge_ref[k] for k in range(4))
    gap = jnp.zeros((1, rows), F32)
    before = [jnp.concatenate([gap, x[:-1]], axis=0) for x in (two, three)]
    after = [jnp.concatenate([x[1:], gap], axis=0) for x in (zero, one)]
    blank = jnp.zeros((blocks, REACH), F32)
    for h in range(2):
        part = slice(h * REACH, (h + 1) * REACH)
        left = jnp.concatenate([before[0][:, part], before[1][:, part], zero[:, part], blank], axis=1)
        right = jnp.concatenate([three[:, part], after[0][:, part], after[1][:, part], blank], axis=1)
        for b in range(blocks):
            out_ref[2 * b + h, 34:35, :] = left[b : b + 1]
            out_ref[2 * b + h, 35:36, :] = right[b : b + 1]

    for p in range(pairs):

        @pl.when(has_above)
        def _():
            rim_down(p).wait_recv()

        @pl.when(has_below)
        def _():
            rim_up(p).wait_recv()

        for k in range(2):
            b = 2 * p + k
            out_ref[2 * b, 38:40, :] = rim_in[0, p, 6:8, k * LANES : (k + 1) * LANES]
            out_ref[2 * b + 1, 32:34, :] = rim_in[1, p, 0:2, k * LANES : (k + 1) * LANES]

    def deal(offset):
        other, device, own = dealt(offset)
        return pltpu.make_async_remote_copy(
            src_ref=out_ref.at[other], dst_ref=got_ref.at[held], send_sem=deal_send.at[offset], recv_sem=deal_recv.at[offset], device_id=device, device_id_type=MESH
        )

    def start_deal(turn, carry):
        offset = jnp.where(turn % 2 == 1, (turn + 1) // 2, lax.rem(sims - turn // 2, sims))
        other, device, own = dealt(offset)

        @pl.when(jnp.logical_not(own))
        def _():
            deal(offset).start()

        @pl.when(own)
        def _():
            pltpu.make_async_copy(out_ref.at[other], got_ref.at[held], deal_recv.at[offset]).start()

        return carry

    def await_deal(offset, carry):
        deal(offset).wait_recv()
        return carry

    lax.fori_loop(0, sims, start_deal, 0)
    for p in range(pairs):
        sent(last, 1, p)
        sent(last + 1, 0, p)

        @pl.when(has_above)
        def _():
            rim_up(p).wait_send()

        @pl.when(has_below)
        def _():
            rim_down(p).wait_send()

    line_ref[...] = jnp.zeros_like(line_ref)
    sums_ref[...] = jnp.zeros_like(sums_ref)
    lax.fori_loop(0, sims, await_deal, 0)

    for d in range(sims):
        s = peer(d)[0]
        own = got_ref[s, 34:36, :]
        partner = 2.0 * got_ref[one_ref[s], 34:36, :] - got_ref[two_ref[s], 34:36, :]
        for side in range(2):
            line_ref[side, d : d + 1, :] = own[side : side + 1]
            line_ref[2 + side, d : d + 1, :] = partner[side : side + 1]
    own_l, own_r, g_l, g_r = (line_ref[k].T for k in range(4))

    def col(x, k):
        return x[k * REACH : (k + 1) * REACH, :]

    flow_ref[0] = 0.5 * col(own_l, 1) * (col(g_l, 2) - col(g_l, 0))
    flow_ref[1] = 0.5 * col(own_r, 1) * (col(g_r, 2) - col(g_r, 0))
    flow_ref[2] = col(g_l, 1)
    flow_ref[3] = col(g_r, 1)
    lane = lax.broadcasted_iota(jnp.int32, (REACH, LANES), 1)
    first, final = lane == 0, lane == LANES - 1
    depth = REACH + 8
    row_spot = pl.ds(pl.multiple_of(half * REACH, REACH), REACH)
    col_spot = pl.ds(pl.multiple_of(chip * LANES, LANES), LANES)

    def home(offset):
        return pltpu.make_async_remote_copy(
            src_ref=est_ref.at[offset],
            dst_ref=result_ref.at[row_spot, col_spot],
            send_sem=home_send.at[offset],
            recv_sem=home_recv.at[offset],
            device_id=peer(offset)[1],
            device_id_type=MESH,
        )

    order = [(k + 1) // 2 if k % 2 else (sims - k // 2) % sims for k in range(sims)]
    for d in order:
        s = peer(d)[0]
        f = got_ref[s]
        g = 2.0 * got_ref[one_ref[s]] - got_ref[two_ref[s]]
        p = f * (pltpu.roll(g, depth - 1, 0) - pltpu.roll(g, 1, 0))
        by_rows = (pltpu.roll(p, depth - 1, 0) - pltpu.roll(p, 1, 0))[:REACH]
        f, g = f[:REACH], g[:REACH]

        def vector(k):
            return jnp.broadcast_to(flow_ref[k, :, d : d + 1], (REACH, LANES))

        ahead = jnp.where(final, vector(3), pltpu.roll(g, LANES - 1, 1))
        behind = jnp.where(first, vector(2), pltpu.roll(g, 1, 1))
        q = 0.5 * f * (ahead - behind)
        ahead = jnp.where(final, vector(1), pltpu.roll(q, LANES - 1, 1))
        behind = jnp.where(first, vector(0), pltpu.roll(q, 1, 1))
        value = 0.25 * by_rows + 0.5 * (ahead - behind)
        if d == 0:
            result_ref[row_spot, col_spot] = value
        else:
            est_ref[d] = value
            home(d).start()
        for o in range(OWNERS):
            sums_ref[o] += jnp.where(owner_ref[s] == o, value, 0.0)
    for o in range(OWNERS):
        tally = jnp.int32(0)
        for s in range(sims):
            tally = tally + (owner_ref[s] == o).astype(jnp.int32)
        sums_ref[o] = sums_ref[o] / jnp.full((REACH, LANES), jnp.maximum(tally, 1).astype(F32))

    swap = pltpu.make_async_remote_copy(
        src_ref=sums_ref, dst_ref=other_ref, send_sem=mean_send, recv_sem=mean_recv, device_id=device_at(me, 2 * chip + 1 - half), device_id_type=MESH
    )
    swap.start()
    wide = LANES // 2

    @pl.when(half == 0)
    def _():
        mean_ref[:, 0:REACH, :] = sums_ref[:, :, 0:wide]

    @pl.when(half == 1)
    def _():
        mean_ref[:, REACH : 2 * REACH, :] = sums_ref[:, :, wide:LANES]

    swap.wait_recv()

    @pl.when(half == 0)
    def _():
        mean_ref[:, REACH : 2 * REACH, :] = other_ref[:, :, 0:wide]

    @pl.when(half == 1)
    def _():
        mean_ref[:, 0:REACH, :] = other_ref[:, :, wide:LANES]

    def await_home(offset, carry):
        pltpu.make_async_remote_copy(
            src_ref=est_ref.at[offset],
            dst_ref=result_ref.at[0:REACH, 0:LANES],
            send_sem=home_send.at[offset],
            recv_sem=home_recv.at[offset],
            device_id=peer(offset)[1],
            device_id_type=MESH,
        ).wait_recv()
        return carry

    def finish_homes(offset, carry):
        home(offset).wait_send()
        return carry

    def finish_deals(offset, carry):
        @pl.when(jnp.logical_not(dealt(offset)[2]))
        def _():
            deal(offset).wait_send()

        return carry

    lax.fori_loop(1, sims, await_home, 0)
    swap.wait_send()
    lax.fori_loop(1, sims, finish_homes, 0)
    lax.fori_loop(0, sims, finish_deals, 0)

    @pl.when(moves)
    def _():
        for kind in range(2):
            for p in range(pairs):
                move(kind, p).wait_send()


def body(maps, weight, beam, pair_one, pair_two, owner):
    rows, cols = weight.shape
    pairs = cols // WIDE
    sims = cols // LANES * 2
    vmem, smem = pl.BlockSpec(memory_space=pltpu.VMEM), pl.BlockSpec(memory_space=pltpu.SMEM)
    est, mean = pl.pallas_call(
        whole_kernel,
        out_shape=(jax.ShapeDtypeStruct((rows, cols), F32), jax.ShapeDtypeStruct((OWNERS, rows, LANES // 2), F32)),
        in_specs=[smem] * 3 + [vmem] * 3,
        out_specs=(vmem, vmem),
        scratch_shapes=[
            pltpu.VMEM((2, pairs, rows, WIDE), F32),
            pltpu.VMEM((2, pairs, rows, WIDE), F32),
            pltpu.VMEM((8, WINDOW), F32),
            pltpu.VMEM((rows, cols), F32),
            pltpu.VMEM((rows, cols), F32),
            pltpu.VMEM((2, pairs, rows, WIDE), F32),
            pltpu.VMEM((STEPS, pairs, REACH, WIDE), F32),
            pltpu.VMEM((STEPS, pairs, REACH, WIDE), F32),
            pltpu.VMEM((2, pairs, 8, WIDE), F32),
            pltpu.VMEM((2, WINDOW, WIDE), BF16),
            pltpu.VMEM((2, WINDOW, WIDE), BF16),
            pltpu.VMEM((2, rows, 6 * rows), BF16),
            pltpu.VMEM((pairs, rows, WINDOW), BF16),
            pltpu.VMEM((pairs, rows, WINDOW), BF16),
            pltpu.VMEM((pairs, 6 * rows, WIDE), BF16),
            pltpu.VMEM((4, cols // LANES, rows), F32),
            pltpu.VMEM((sims, REACH + 8, LANES), F32),
            pltpu.VMEM((sims, REACH + 8, LANES), F32),
            pltpu.VMEM((4, LANES, LANES), F32),
            pltpu.VMEM((4, REACH, LANES), F32),
            pltpu.VMEM((sims, REACH, LANES), F32),
            pltpu.VMEM((OWNERS, REACH, LANES), F32),
            pltpu.VMEM((OWNERS, REACH, LANES), F32),
            pltpu.SemaphoreType.DMA((2, STEPS, pairs)),
            pltpu.SemaphoreType.DMA((2, STEPS, pairs)),
            pltpu.SemaphoreType.DMA((2, pairs)),
            pltpu.SemaphoreType.DMA((2, pairs)),
            pltpu.SemaphoreType.DMA((sims,)),
            pltpu.SemaphoreType.DMA((sims,)),
            pltpu.SemaphoreType.DMA((sims,)),
            pltpu.SemaphoreType.DMA((sims,)),
            pltpu.SemaphoreType.DMA((2, pairs)),
            pltpu.SemaphoreType.DMA((2, pairs)),
            pltpu.SemaphoreType.DMA,
            pltpu.SemaphoreType.DMA,
        ],
        compiler_params=pltpu.CompilerParams(collective_id=0, has_side_effects=True),
    )(pair_one, pair_two, owner, maps[0], weight, beam.reshape(1, TAPS))
    return est[None], mean


def solution(mesh):
    split = Mesh(mesh.devices.reshape(16, 2, mesh.shape["rows"]), ("chips", "core", "rows"))
    sims = ("chips", "core")
    return jax.shard_map(
        body,
        mesh=split,
        in_specs=(P(sims, "rows", None), P("rows", None), P(), P(), P(), P()),
        out_specs=(P(sims, "rows", None), P(None, "rows", sims)),
        check_vma=False,
    )
```
